32 devices in a mesh: dp: 8 (over z, x), sp: 4 (over y, core).
Axes of the slice: x: 2, y: 2, z: 4, core: 2. Of those that a mesh axis runs over, the one named last changes fastest.
Arguments:
- tokens: bfloat16 [8192, 1024], P(('dp', 'sp')), may hold values from -6 to 6
- segment_ids: int32 [8, 1024], P('dp'), may hold values from 0 to 15, as said below
- norm_gain: float32 [1024], replicated, may hold values from 0.25 to 1.75
- norm_bias: float32 [1024], replicated, may hold values from -4 to 4
- qkv_weight: bfloat16 [3, 1024, 1024], replicated, may hold values from -0.25 to 0.25
- out_weight: bfloat16 [1024, 1024], replicated, may hold values from -0.375 to 0.375
- in_weight: bfloat16 [1024, 4096], replicated, may hold values from -0.1875 to 0.1875
- in_bias: float32 [4096], replicated, may hold values from -6 to 6
- proj_weight: bfloat16 [4096, 1024], replicated, may hold values from -0.09375 to 0.09375
- proj_bias: float32 [1024], replicated, may hold values from -6 to 6
- cotangent: bfloat16 [8192, 1024], P(('dp', 'sp')), may hold values from -6 to 6
Outputs:
- out: bfloat16 [8192, 1024], P(('dp', 'sp'))
- d_tokens: float32 [8192, 1024], P(('dp', 'sp'))
- g_norm_gain: float32 [1024], replicated
- g_norm_bias: float32 [1024], replicated
- g_qkv: float32 [3, 1024, 1024], P(None, 'dp', 'sp')
- g_out: float32 [1024, 1024], P('sp', 'dp')
- g_in: float32 [1024, 4096], P('dp', 'sp')
- g_in_bias: float32 [4096], replicated
- g_proj: float32 [4096, 1024], P('sp', 'dp')
- g_proj_bias: float32 [1024], replicated
The draws below stay inside these ranges and needn't reach their ends.
Inputs may be any that keep to these rules, and one draw needn't show every extreme that they name: `segment_ids`: within each group the protein numbers never fall; every protein is one run of 1 to 512 positions and one protein of every group has exactly 512; all 16 numbers occur in every group; the last protein of every group is a single position.
All inputs are finite; a program needn't handle non-finite values.
Results may differ from the reference program's by a relative error of at most 0.012.
The reference program's roundings to bfloat16 on the way count: a program that leaves them out, or rounds other values in their place, can miss the bound.
Values may be sent and summed in bfloat16 or wider, within the bound.
A program may use at most 192 MiB of HBM per device.

```python
import math
import jax
import jax.numpy as jnp
from jax import lax

D = 1024
H = 16
HD = 64
ROT = 32
FF = 4096
NSEG = 16
GROUP = 1024
GROUPS = 8
TOKENS = 8192
MOST = 512


def group_layout(group_key):
    cut_key, slot_key = jax.random.split(group_key)
    rest_len = GROUP - MOST
    free_cuts = jax.random.permutation(cut_key, rest_len - 2)[:NSEG - 3] + 1
    cut_points = jnp.sort(jnp.concatenate([free_cuts.astype(jnp.int32), jnp.full((1,), rest_len - 1, jnp.int32)])).astype(jnp.int32)
    edge_points = jnp.concatenate([jnp.zeros((1,), jnp.int32), cut_points, jnp.full((1,), rest_len, jnp.int32)])
    short_lengths = edge_points[1:] - edge_points[:-1]
    long_slot = jax.random.randint(slot_key, (), 0, NSEG - 1)
    slot_index = jnp.arange(NSEG, dtype=jnp.int32)
    before_slot = jnp.take(short_lengths, jnp.clip(slot_index, 0, NSEG - 2))
    after_slot = jnp.take(short_lengths, jnp.clip(slot_index - 1, 0, NSEG - 2))
    lengths = jnp.where(slot_index < long_slot, before_slot, jnp.where(slot_index == long_slot, MOST, after_slot)).astype(jnp.int32)
    start_points = (jnp.cumsum(lengths) - lengths).astype(jnp.int32)
    positions = jnp.arange(GROUP, dtype=jnp.int32)
    protein_ids = jnp.sum((positions[:, None] >= start_points[None, 1:]).astype(jnp.int32), axis=1).astype(jnp.int32)
    return protein_ids


def draw_segment_ids(key, part):
    group_keys = jax.random.split(jax.random.fold_in(key, 11), GROUPS)
    return jax.vmap(group_layout)(group_keys)


def spiked(drawn, key, source, target, shards_of, factor):
    def block_of(position):
        return (jnp.arange(drawn.shape[position]) // (drawn.shape[position] // shards_of)).reshape((-1,) + (1,) * (drawn.ndim - 1 - position))

    near = jax.random.permutation(key, shards_of)[block_of(target)]
    other_side = (block_of(target) + shards_of // 2) % shards_of
    return jnp.where((block_of(source) == near) | (block_of(source) == other_side), factor * drawn, drawn)


def block_levels(rng, dims, pieces, low, largest):
    factor_of, own = 1.0, jax.random.fold_in(rng, 6)
    for dim, parts in pieces:
        draws = jnp.exp(jax.random.uniform(jax.random.fold_in(own, dim), (parts,), jnp.float32, low / len(pieces), largest / len(pieces)))
        factor_of = factor_of * jnp.repeat(draws, dims[dim] // parts).reshape([-1 if axis == dim else 1 for axis in range(len(dims))])
    return factor_of


def noise(own_key, shape, scale, most, shards=(), kind=jnp.bfloat16):
    values = scale * jax.random.normal(own_key, shape, jnp.float32)
    if shards:
        values = values * block_levels(own_key, shape, shards, -0.22, 0.18)
    return jnp.clip(values, -most, most).astype(kind)


def noise_with(stream_key, extent, spread, reach, cuts, heavy, held_as=jnp.bfloat16):
    drawn = spread * jax.random.normal(stream_key, extent, jnp.float32)
    if cuts:
        drawn = drawn * block_levels(stream_key, extent, cuts, -0.22, 0.18)
    return jnp.clip(spiked(drawn, jax.random.fold_in(stream_key, 3), *heavy), -reach, reach).astype(held_as)


def setup_inputs(seed: int = 0) -> dict:
    arg_keys = jax.random.split(jax.random.key(seed), 12)
    tokens = noise(arg_keys[0], (TOKENS, D), 1.0, 6.0, ((0, 32),))
    segment_ids = draw_segment_ids(jax.random.fold_in(arg_keys[11], 71), 0)
    norm_gain = jnp.clip(1.0 + 0.15 * jax.random.normal(arg_keys[2], (D,), jnp.float32), 0.25, 1.75)
    norm_bias = noise(arg_keys[3], (D,), 0.3, 4.0, (), jnp.float32)
    qkv_weight = noise(arg_keys[4], (3, D, H * HD), (D // 2) ** -0.5, 0.25)
    out_weight = noise(arg_keys[5], (H * HD, D), (4 * HD) ** -0.5, 0.375)
    in_weight = noise(arg_keys[6], (D, FF), D ** -0.5, 0.1875)
    in_bias = noise(arg_keys[7], (FF,), 0.5, 6.0, (), jnp.float32)
    proj_weight = noise(arg_keys[8], (FF, D), FF ** -0.5, 0.09375)
    proj_bias = noise(arg_keys[9], (D,), 0.5, 6.0, (), jnp.float32)
    cotangent = noise_with(arg_keys[10], (TOKENS, D), 1.0, 6.0, ((0, 32),), (0, 1, 32, 2.75))
    return {"tokens": tokens, "segment_ids": segment_ids, "norm_gain": norm_gain, "norm_bias": norm_bias, "qkv_weight": qkv_weight, "out_weight": out_weight, "in_weight": in_weight, "in_bias": in_bias, "proj_weight": proj_weight, "proj_bias": proj_bias, "cotangent": cotangent}


NEG_FILL = -1e+30

@jax.custom_vjp
def low(v):
    return lax.optimization_barrier(v.astype(jnp.bfloat16)).astype(jnp.float32)

@jax.custom_vjp
def low_back(v):
    return v

def low_keep(v):
    return (low(v), None)

def low_pass(kept, grad):
    return (grad,)

def back_keep(v):
    return (v, None)

def back_low(kept, grad):
    return (low(grad),)
low.defvjp(low_keep, low_pass)
low_back.defvjp(back_keep, back_low)

def hp_dot(left_side, right_side):
    return jnp.dot(left_side, right_side, precision=lax.Precision.HIGHEST, preferred_element_type=jnp.float32)

def normalize(row_values, norm_gain, norm_bias):
    row_mean = lax.optimization_barrier(jnp.mean(row_values, axis=-1, keepdims=True))
    centered = row_values - row_mean
    variance = lax.optimization_barrier(jnp.mean(centered * centered, axis=-1, keepdims=True))
    return centered * lax.rsqrt(variance + 1e-05) * norm_gain + norm_bias

def gelu_tanh(values):
    return 0.5 * values * (1.0 + jnp.tanh(0.7978845608028654 * (values + 0.044715 * values * values * values)))

def angles(positions):
    half_rot = ROT // 2
    frequency = 10000.0 ** (-2.0 * jnp.arange(half_rot, dtype=jnp.float32) / ROT)
    turned = positions.astype(jnp.float32)[:, None] * frequency[None, :]
    return (jnp.cos(turned)[:, None, :], jnp.sin(turned)[:, None, :])

def rotate(values, cosine, sine_part):
    row_count = values.shape[0]
    half_rot = ROT // 2
    shaped = values.reshape(row_count, -1, HD)
    first_part = shaped[:, :, :half_rot]
    second = shaped[:, :, half_rot:ROT]
    untouched = shaped[:, :, ROT:]
    turned = jnp.concatenate([first_part * cosine - second * sine_part, second * cosine + first_part * sine_part, untouched], axis=-1)
    return turned.reshape(row_count, -1)

def positions_of(segment_row):
    matches = segment_row[:, None] == jnp.arange(NSEG, dtype=jnp.int32)[None, :]
    counts = lax.optimization_barrier(jnp.sum(matches.astype(jnp.int32), axis=0, dtype=jnp.int32))
    starts_row = (jnp.cumsum(counts) - counts).astype(jnp.int32)
    begin_at = lax.optimization_barrier(jnp.sum(jnp.where(matches, starts_row[None, :], 0), axis=1, dtype=jnp.int32))
    return jnp.arange(segment_row.shape[0], dtype=jnp.int32) - begin_at

def reference(tokens, segment_ids, norm_gain, norm_bias, qkv_weight, out_weight, in_weight, in_bias, proj_weight, proj_bias, cotangent):
    positions = jax.vmap(positions_of)(segment_ids).reshape(-1)
    cosine, sine_part = angles(positions)
    block_rows = min(512, GROUP)
    block_count = GROUP // block_rows
    score_scale = 1.0 / math.sqrt(HD)
    seg_blocks = segment_ids.reshape(GROUPS * block_count, block_rows)
    numbers = jnp.arange(GROUPS * block_count, dtype=jnp.int32)

    def forward(row_values, ln_gain, ln_shift, w_qkv, w_mix, w_in, b_in, w_proj, b_proj):
        normed = low(normalize(row_values, ln_gain, ln_shift))
        queries = low(rotate(low_back(hp_dot(normed, w_qkv[0])), cosine, sine_part))
        key_rows = low(rotate(low_back(hp_dot(normed, w_qkv[1])), cosine, sine_part))
        value_rows = low(low_back(hp_dot(normed, w_qkv[2])))
        key_heads = key_rows.reshape(GROUPS, GROUP, H, HD)
        value_heads = value_rows.reshape(GROUPS, GROUP, H, HD)
        query_blocks = queries.reshape(GROUPS * block_count, block_rows, H, HD)

        def attend(block_items):
            query_block, seg_block, block_number = block_items
            group_number = block_number // block_count
            block_start = block_number % block_count * block_rows
            key_group = lax.dynamic_index_in_dim(key_heads, group_number, 0, keepdims=False)
            value_group = lax.dynamic_index_in_dim(value_heads, group_number, 0, keepdims=False)
            seg_group = lax.dynamic_index_in_dim(segment_ids, group_number, 0, keepdims=False)
            raw_scores = jnp.einsum('qhd,khd->hqk', query_block, key_group, precision=lax.Precision.HIGHEST)
            query_index = block_start + jnp.arange(block_rows, dtype=jnp.int32)
            key_index = jnp.arange(GROUP, dtype=jnp.int32)
            allowed = (seg_block[:, None] == seg_group[None, :]) & (key_index[None, :] <= query_index[:, None])
            scores = jnp.where(allowed[None], low_back(raw_scores * score_scale), NEG_FILL)
            log_total = jax.nn.logsumexp(scores, axis=-1, keepdims=True)
            weights = low(jnp.exp(scores - log_total))
            mixed_block = jnp.einsum('hqk,khd->qhd', weights, value_group, precision=lax.Precision.HIGHEST)
            return low(low_back(mixed_block))
        mixed = lax.map(jax.checkpoint(attend), (query_blocks, seg_blocks, numbers)).reshape(GROUPS * GROUP, H * HD)
        attention = hp_dot(mixed, w_mix)
        pre_act = low_back(hp_dot(normed, w_in) + b_in)
        hidden = low(gelu_tanh(pre_act))
        return row_values + attention + hp_dot(hidden, w_proj) + b_proj
    primal, pull_back = jax.vjp(forward, tokens.astype(jnp.float32), norm_gain, norm_bias, qkv_weight.astype(jnp.float32), out_weight.astype(jnp.float32), in_weight.astype(jnp.float32), in_bias, proj_weight.astype(jnp.float32), proj_bias)
    grads = pull_back(cotangent.astype(jnp.float32))
    return (primal.astype(jnp.bfloat16), grads[0], grads[1], grads[2], grads[3], grads[4], grads[5], grads[6], grads[7], grads[8])
```

```python
import math

import jax
import jax.numpy as jnp
from jax import lax
from jax.sharding import PartitionSpec as P

HD = 64
ROT = 32
NSEG = 16

NEG_FILL = -1e30
F32 = jnp.float32
BF16 = jnp.bfloat16


def gelu_tanh(values):
    return (
        0.5
        * values
        * (1.0 + jnp.tanh(0.7978845608028654 * (values + 0.044715 * values * values * values)))
    )


def angles(positions):
    half_rot = ROT // 2
    frequency = 10000.0 ** (-2.0 * jnp.arange(half_rot, dtype=F32) / ROT)
    turned = positions.astype(F32)[:, None] * frequency[None, :]
    return (jnp.cos(turned)[:, None, :], jnp.sin(turned)[:, None, :])


def rotate(values, cosine, sine_part):
    row_count = values.shape[0]
    half_rot = ROT // 2
    shaped = values.reshape(row_count, -1, HD)
    first_part = shaped[:, :, :half_rot]
    second = shaped[:, :, half_rot:ROT]
    untouched = shaped[:, :, ROT:]
    turned = jnp.concatenate(
        [
            first_part * cosine - second * sine_part,
            second * cosine + first_part * sine_part,
            untouched,
        ],
        axis=-1,
    )
    return turned.reshape(row_count, -1)


def positions_of(segment_row):
    matches = segment_row[:, None] == jnp.arange(NSEG, dtype=jnp.int32)[None, :]
    counts = jnp.sum(matches.astype(jnp.int32), axis=0, dtype=jnp.int32)
    starts_row = jnp.cumsum(counts) - counts
    begin_at = jnp.sum(jnp.where(matches, starts_row[None, :], 0), axis=1, dtype=jnp.int32)
    return jnp.arange(segment_row.shape[0], dtype=jnp.int32) - begin_at


def attention_both(q, k, v, gm, seg):
    group_len = q.shape[0]
    scale = 1.0 / math.sqrt(HD)
    raw = jnp.einsum("qhd,khd->hqk", q, k, preferred_element_type=F32)
    index = jnp.arange(group_len, dtype=jnp.int32)
    allowed = (seg[:, None] == seg[None, :]) & (index[None, :] <= index[:, None])
    scores = jnp.where(allowed[None], raw * scale, NEG_FILL)
    top = jnp.max(scores, axis=-1, keepdims=True)
    expd = jnp.exp(scores - top)
    p = expd / jnp.sum(expd, axis=-1, keepdims=True)
    p_low = p.astype(BF16)
    mixed = jnp.einsum("hqk,khd->qhd", p_low, v, preferred_element_type=F32).astype(BF16)
    gp = jnp.einsum("qhd,khd->hqk", gm, v, preferred_element_type=F32)
    inner = jnp.sum(p * gp, axis=-1, keepdims=True)
    gs = (p * (gp - inner)).astype(BF16)
    gq = jnp.einsum("hqk,khd->qhd", gs, k, preferred_element_type=F32) * scale
    gk = jnp.einsum("hqk,qhd->khd", gs, q, preferred_element_type=F32) * scale
    gv = jnp.einsum("hqk,qhd->khd", p_low, gm, preferred_element_type=F32)
    return mixed, gq, gk, gv


def per_device(
    tokens,
    segment_ids,
    norm_gain,
    norm_bias,
    qkv_weight,
    out_weight,
    in_weight,
    in_bias,
    proj_weight,
    proj_bias,
    cotangent,
):
    tok_rows, width = tokens.shape
    n_sp = lax.axis_size("sp")
    j = lax.axis_index("sp")
    hw = qkv_weight.shape[2] // n_sp
    fw = in_weight.shape[1] // n_sp
    seg = segment_ids[0]
    group_len = seg.shape[0]
    positions = positions_of(seg)
    cosine, sine = angles(positions)

    rows = tokens.astype(F32)
    cot_own = cotangent.astype(F32)
    mean = jnp.mean(rows, axis=-1, keepdims=True)
    centered = rows - mean
    var = jnp.mean(centered * centered, axis=-1, keepdims=True)
    inv = lax.rsqrt(var + 1e-05)
    xhat = centered * inv
    normed_own = (xhat * norm_gain + norm_bias).astype(BF16)

    normed = lax.all_gather(normed_own, "sp", axis=0, tiled=True)
    cot = lax.all_gather(cotangent, "sp", axis=0, tiled=True)

    w_qkv = lax.dynamic_slice_in_dim(qkv_weight, j * hw, hw, 2)
    w_out = lax.dynamic_slice_in_dim(out_weight, j * hw, hw, 0)
    w_in = lax.dynamic_slice_in_dim(in_weight, j * fw, fw, 1)
    b_in = lax.dynamic_slice_in_dim(in_bias, j * fw, fw, 0)
    w_proj = lax.dynamic_slice_in_dim(proj_weight, j * fw, fw, 0)

    pre = jnp.dot(normed, w_in, preferred_element_type=F32) + b_in
    hidden, gelu_pull = jax.vjp(gelu_tanh, pre)
    hidden = hidden.astype(BF16)
    g_proj = jnp.einsum("tf,td->fd", hidden, cot, preferred_element_type=F32)
    grad_hidden = jnp.einsum("td,fd->tf", cot, w_proj, preferred_element_type=F32)
    grad_pre = gelu_pull(grad_hidden)[0].astype(BF16)
    g_in = jnp.einsum("td,tf->df", normed, grad_pre, preferred_element_type=F32)
    g_in_bias = jnp.sum(grad_pre.astype(F32), axis=0)

    projected = jnp.einsum("td,cde->cte", normed, w_qkv, preferred_element_type=F32)
    q = rotate(projected[0], cosine, sine).astype(BF16).reshape(group_len, -1, HD)
    k = rotate(projected[1], cosine, sine).astype(BF16).reshape(group_len, -1, HD)
    v = projected[2].astype(BF16).reshape(group_len, -1, HD)
    grad_mixed = jnp.einsum("td,ed->te", cot, w_out, preferred_element_type=F32).astype(BF16)
    mixed, gq, gk, gv = attention_both(q, k, v, grad_mixed.reshape(group_len, -1, HD), seg)
    mixed = mixed.reshape(group_len, -1)
    gq = rotate(gq.reshape(group_len, -1), cosine, -sine).astype(BF16)
    gk = rotate(gk.reshape(group_len, -1), cosine, -sine).astype(BF16)
    gv = gv.reshape(group_len, -1).astype(BF16)
    g_out = jnp.einsum("te,td->ed", mixed, cot, preferred_element_type=F32)
    grads = jnp.stack([gq, gk, gv])
    g_qkv = jnp.einsum("td,cte->cde", normed, grads, preferred_element_type=F32)

    part_out = jnp.dot(mixed, w_out, preferred_element_type=F32) + jnp.dot(
        hidden, w_proj, preferred_element_type=F32
    )
    part_gn = jnp.einsum("cte,cde->td", grads, w_qkv, preferred_element_type=F32) + jnp.einsum(
        "tf,df->td", grad_pre, w_in, preferred_element_type=F32
    )
    block_out = lax.psum_scatter(part_out.astype(BF16), "sp", scatter_dimension=0, tiled=True)
    grad_normed = lax.psum_scatter(
        part_gn.astype(BF16), "sp", scatter_dimension=0, tiled=True
    ).astype(F32)

    out = rows + block_out.astype(F32) + proj_bias
    gain_grad = jnp.sum(grad_normed * xhat, axis=0)
    shift_grad = jnp.sum(grad_normed, axis=0)
    e = grad_normed * norm_gain
    d_tokens = cot_own + inv * (
        e
        - jnp.mean(e, axis=-1, keepdims=True)
        - xhat * jnp.mean(e * xhat, axis=-1, keepdims=True)
    )
    proj_bias_grad = jnp.sum(cot_own, axis=0)

    g_qkv = lax.psum_scatter(g_qkv.astype(BF16), "dp", scatter_dimension=1, tiled=True)
    g_out = lax.psum_scatter(g_out.astype(BF16), "dp", scatter_dimension=1, tiled=True)
    g_in = lax.psum_scatter(g_in.astype(BF16), "dp", scatter_dimension=0, tiled=True)
    g_proj = lax.psum_scatter(g_proj.astype(BF16), "dp", scatter_dimension=1, tiled=True)
    bias_full = lax.dynamic_update_slice_in_dim(
        jnp.zeros(in_bias.shape, F32), g_in_bias, j * fw, 0
    )
    vectors = lax.psum((gain_grad, shift_grad, bias_full, proj_bias_grad), ("dp", "sp"))
    return (
        out.astype(BF16),
        d_tokens,
        vectors[0],
        vectors[1],
        g_qkv.astype(F32),
        g_out.astype(F32),
        g_in.astype(F32),
        vectors[2],
        g_proj.astype(F32),
        vectors[3],
    )


def solution(mesh):
    placed = (
        P(("dp", "sp"), None),
        P("dp", None),
        P(),
        P(),
        P(),
        P(),
        P(),
        P(),
        P(),
        P(),
        P(("dp", "sp"), None),
    )
    return jax.shard_map(
        per_device,
        mesh=mesh,
        in_specs=placed,
        out_specs=(
            P(("dp", "sp"), None),
            P(("dp", "sp"), None),
            P(),
            P(),
            P(None, "dp", "sp"),
            P("sp", "dp"),
            P("dp", "sp"),
            P(),
            P("sp", "dp"),
            P(),
        ),
        check_vma=False,
    )
```

```python
import functools
import math

import jax
import jax.numpy as jnp
from jax import lax
from jax.experimental import pallas as pl
from jax.experimental.pallas import tpu as pltpu
from jax.sharding import PartitionSpec as P

HD = 64
ROT = 32
NSEG = 16
LANES = 128
QB = 256
CH = 16

NEG_FILL = -1e30
F32 = jnp.float32
BF16 = jnp.bfloat16
MESH = pl.DeviceIdType.MESH

NN = (((1,), (0,)), ((), ()))
NT = (((1,), (1,)), ((), ()))
TN = (((0,), (0,)), ((), ()))

C0 = 0.7978845608028654
C1 = 0.044715


def dot(left, right, dims):
    return lax.dot_general(left, right, dims, preferred_element_type=F32)


def copy_to(src, dst, send, recv, target):
    return pltpu.make_async_remote_copy(
        src_ref=src, dst_ref=dst, send_sem=send, recv_sem=recv, device_id=target, device_id_type=MESH
    )


def chunks(count, step, fn):
    def one(i, carry):
        fn(pl.ds(pl.multiple_of(i * step, step), step))
        return carry

    lax.fori_loop(0, count // step, one, 0)


def block_kernel(sizes, *refs):
    n_in, n_out, names = sizes["n_in"], sizes["n_out"], sizes["scratch"]
    (tok_h, cot_h, segc, segr, tab_c, tab_s, gain, shift, b_in, b_proj, wqkv_h, wout_h, win_h, wproj_h) = refs[:n_in]
    (out_o, dtok_o, sum_p, sum_i, sum_a, vec_o, inb_o) = refs[n_in : n_in + n_out]
    sc = dict(zip(names, refs[n_in + n_out :]))
    T, D, G, S, DP = sizes["T"], sizes["D"], sizes["G"], sizes["S"], sizes["DP"]
    NX, NZ, NY = sizes["NX"], sizes["NZ"], sizes["NY"]
    HW, FW, DB, ZW, CW = sizes["HW"], sizes["FW"], sizes["DB"], sizes["ZW"], sizes["CW"]
    window = G // 2
    scale = 1.0 / math.sqrt(HD)

    nrm, cot, hid, dgel, gpre = sc["nrm"], sc["cot"], sc["hid"], sc["dgel"], sc["gpre"]
    q_s, k_s, v_s, gm, mix = sc["q"], sc["k"], sc["v"], sc["gm"], sc["mix"]
    tmp, acc, xs, xr, zr = sc["tmp"], sc["acc"], sc["xs"], sc["xr"], sc["zr"]
    outs = (sum_p, sum_i, sum_a)

    dp = lax.axis_index("dp")
    sp = lax.axis_index("sp")
    z, x, y, c = dp // NX, dp % NX, sp // 2, sp % 2
    sib = (dp, y * 2 + 1 - c)

    def at_y(y_):
        return (dp, y_ * 2 + c)

    def rows(y_, c_):
        return pl.ds(pl.multiple_of((y_ * 2 + c_) * T, T), T)

    own = rows(y, c)

    ld = sc["ld_sem"]
    load_tok = pltpu.make_async_copy(tok_h, sc["tok"], ld.at[0])
    load_cot = pltpu.make_async_copy(cot_h, cot.at[own, :], ld.at[1])
    fcols = pl.ds(pl.multiple_of(sp * FW, LANES), FW)
    hcols = pl.ds(pl.multiple_of(sp * HW, LANES), HW)
    load_in = pltpu.make_async_copy(win_h.at[:, fcols], sc["win"], ld.at[2])
    load_qkv = pltpu.make_async_copy(wqkv_h.at[:, :, hcols], sc["wqkv"], ld.at[3])
    load_proj = pltpu.make_async_copy(wproj_h.at[fcols, :], sc["wproj"], ld.at[4])
    load_out = pltpu.make_async_copy(wout_h.at[hcols, :], sc["wout"], ld.at[5])
    for load in (load_tok, load_cot, load_in, load_qkv, load_proj, load_out):
        load.start()

    barrier = pltpu.get_barrier_semaphore()
    for d in range(1, DP):
        pl.semaphore_signal(barrier, inc=1, device_id=((dp + d) % DP, sp), device_id_type=MESH)
    for d in range(1, S):
        pl.semaphore_signal(barrier, inc=1, device_id=(dp, (sp + d) % S), device_id_type=MESH)

    vacc = sc["vacc"]
    vacc[...] = jnp.zeros_like(vacc)

    def fold(value):
        return jnp.sum(value.reshape(CH // 8, 8, value.shape[-1]), axis=0)

    def stats(r):
        row = sc["tok"][r, :].astype(F32)
        mean = jnp.mean(row, axis=-1, keepdims=True)
        cent = row - mean
        var = jnp.mean(cent * cent, axis=-1, keepdims=True)
        inv = lax.rsqrt(var + 1e-05)
        return row, cent * inv, inv

    load_tok.wait()

    def norm_chunk(r):
        _, xhat, _ = stats(r)
        sc["nown"][r, :] = (xhat * gain[...] + shift[...]).astype(BF16)

    chunks(T, CH, norm_chunk)
    nrm[own, :] = sc["nown"][...]

    pl.semaphore_wait(barrier, DP - 1 + S - 1)

    def target(k):
        if k == NZ - 1:
            return z
        low = z < NZ // 2
        zz = jnp.where(low, z, NZ - 1 - z)
        v = NZ - 1 - k
        w = jnp.where(v <= zz, v - 1, v)
        return jnp.where(low, w, NZ - 1 - w)

    def zcols(k):
        return pl.ds(pl.multiple_of(target(k) * ZW, LANES), ZW)

    ns, nr, cs, cr = sc["ns"], sc["nr"], sc["cs"], sc["cr"]

    def send_rows(buf, view, ssem, rsem, slot, target_dev):
        cp = copy_to(buf.at[view], buf.at[view], ssem.at[slot], rsem.at[slot], target_dev)
        cp.start()
        return cp

    def got(buf, view, ssem, rsem, slot):
        copy_to(buf.at[view], buf.at[view], ssem.at[slot], rsem.at[slot], sib).wait_recv()

    sent = []
    for d in range(1, NY):
        sent.append(send_rows(nrm, (own, slice(None)), ns, nr, d, at_y((y + d) % NY)))
    sent.append(send_rows(nrm, (own, slice(None)), ns, nr, 0, sib))
    load_cot.wait()
    for k in range(NZ):
        for d in range(1, NY):
            sent.append(send_rows(cot, (own, zcols(k)), cs.at[k], cr.at[k], d, at_y((y + d) % NY)))
        sent.append(send_rows(cot, (own, zcols(k)), cs.at[k], cr.at[k], 0, sib))

    def relay_cot(k):
        for d in range(1, NY):
            view = (rows((y + NY - d) % NY, c), zcols(k))
            got(cot, view, cs.at[k], cr.at[k], d)
            sent.append(send_rows(cot, view, cs.at[k], cr.at[k], NY - 1 + d, sib))

    def wait_cot(k):
        got(cot, (rows(y, 1 - c), zcols(k)), cs.at[k], cr.at[k], 0)
        for d in range(1, NY):
            got(cot, (rows((y + NY - d) % NY, 1 - c), zcols(k)), cs.at[k], cr.at[k], NY - 1 + d)

    lane = lax.broadcasted_iota(jnp.int32, (T, LANES), 1)
    low_half = (lane % HD) < (ROT // 2)

    def turn(u, r, sign):
        partner = jnp.where(
            low_half[: u.shape[0]],
            pltpu.roll(u, LANES - ROT // 2, 1),
            pltpu.roll(u, ROT // 2, 1),
        )
        return u * tab_c[r, :] + sign * (partner * tab_s[r, :])

    bias_row = b_in[:, fcols]

    def forward(r):
        xb = nrm[r, :]
        tmp[:T, :] = dot(xb, sc["win"][...], NN)

        def gelu_chunk(i, carry):
            rr = pl.ds(pl.multiple_of(i * CH, CH), CH)
            gr = pl.ds(pl.multiple_of(r.start + i * CH, CH), CH)
            a = tmp[rr, :] + bias_row
            a2 = a * a
            th = jnp.tanh(C0 * (a + C1 * a2 * a))
            half = 0.5 * (1.0 + th)
            hid[gr, :] = (a * half).astype(BF16)
            dgel[gr, :] = half + 0.5 * a * (1.0 - th * th) * (C0 * (1.0 + 3.0 * C1 * a2))
            return carry

        lax.fori_loop(0, T // CH, gelu_chunk, 0)
        for part in range(3):
            u = dot(xb, sc["wqkv"][part], NN)
            for t in range(HW // LANES):
                cols = slice(t * LANES, (t + 1) * LANES)
                if part == 0:
                    q_s[r, cols] = turn(u[:, cols], r, 1.0).astype(BF16) * jnp.asarray(scale, BF16)
                elif part == 1:
                    k_s[r, cols] = turn(u[:, cols], r, 1.0).astype(BF16)
                else:
                    v_s[r, cols] = u[:, cols].astype(BF16)

    load_in.wait()
    load_qkv.wait()
    forward(own)
    got(nrm, (rows(y, 1 - c), slice(None)), ns, nr, 0)
    forward(rows(y, 1 - c))
    for d in range(1, NY):
        view = (rows((y + NY - d) % NY, c), slice(None))
        got(nrm, view, ns, nr, d)
        sent.append(send_rows(nrm, view, ns, nr, NY - 1 + d, sib))
        forward(view[0])
    relay_cot(0)
    for d in range(1, NY):
        view = (rows((y + NY - d) % NY, 1 - c), slice(None))
        got(nrm, view, ns, nr, NY - 1 + d)
        forward(view[0])
    relay_cot(1)

    xss, xrs, zss, zrs = sc["xss"], sc["xrs"], sc["zss"], sc["zrs"]

    def x_copy(g, k, d):
        return copy_to(
            xs.at[g, k, d - 1], xr.at[g, k, d - 1], xss.at[g, k, d - 1], xrs.at[g, k, d - 1],
            (z * NX + (x + d) % NX, sp),
        )

    def hand_out(g, k):
        for d in range(1, NX):
            xs[g, k, d - 1] = tmp[pl.ds(pl.multiple_of((x + d) % NX * DB, DB), DB), :].astype(BF16)
            x_copy(g, k, d).start()
        acc[g, k] = tmp[pl.ds(pl.multiple_of(x * DB, DB), DB), :]

    def z_slot(zt, nz, up):
        return jnp.where(up, zt, jnp.where(zt == nz, NZ, zt))

    def z_copy(g, k):
        zt = target(k)
        up = zt > z
        nz = jnp.where(up, z + 1, z - 1)
        slot = z_slot(zt, nz, up)
        return copy_to(
            xs.at[g, k, 0], zr.at[g, slot], zss.at[g, k], zrs.at[g, slot], (nz * NX + x, sp)
        )

    def z_got(g, slot):
        copy_to(xs.at[g, 0, 0], zr.at[g, slot], zss.at[g, 0], zrs.at[g, slot], sib).wait_recv()

    def is_source(k):
        up = target(k) > z
        return jnp.where(up, z == 0, z == NZ - 1)

    def x_add(g, k):
        for d in range(1, NX):
            x_copy(g, k, d).wait()

        def add(r):
            total = acc[g, k, r, :]
            for d in range(1, NX):
                total = total + xr[g, k, d - 1, r, :].astype(F32)
            acc[g, k, r, :] = total

        chunks(DB, CH, add)

    def z_send(g, k):
        xs[g, k, 0] = acc[g, k].astype(BF16)
        z_copy(g, k).start()

    def z_first(g, k):
        @pl.when(is_source(k))
        def _():
            z_send(g, k)

    def z_next(g, k):
        @pl.when(jnp.logical_not(is_source(k)))
        def _():
            slot = target(k)
            z_got(g, slot)

            def add(r):
                acc[g, k, r, :] = acc[g, k, r, :] + zr[g, slot, r, :].astype(F32)

            chunks(DB, CH, add)
            z_send(g, k)

    def z_last(g):
        k = NZ - 1
        outs[g][...] = acc[g, k]

        @pl.when(z > 0)
        def _():
            z_got(g, z)
            outs[g][...] = outs[g][...] + zr[g, z].astype(F32)

        @pl.when(z < NZ - 1)
        def _():
            z_got(g, NZ)
            outs[g][...] = outs[g][...] + zr[g, NZ].astype(F32)

        for j in range(NZ - 1):
            z_copy(g, j).wait_send()

    def tick(n):
        g, k = n // NZ, n % NZ
        if n < 3 * NZ:
            x_add(g, k)
            if k < NZ - 1:
                z_first(g, k)
        if n > 0:
            g, k = (n - 1) // NZ, (n - 1) % NZ
            if k < NZ - 1:
                z_next(g, k)
            else:
                z_last(g)

    for k in range(NZ):
        if k + 2 < NZ:
            relay_cot(k + 2)
        wait_cot(k)
        tmp[:ZW, :] = dot(cot[:, zcols(k)], hid[...], TN)
        hand_out(0, k)

    load_proj.wait()
    load_out.wait()

    def backward(r):
        cb = cot[r, :]
        tmp[:T, :] = dot(cb, sc["wproj"][...], NT)

        def chunk(i, carry):
            rr = pl.ds(pl.multiple_of(i * CH, CH), CH)
            gr = pl.ds(pl.multiple_of(r.start + i * CH, CH), CH)
            low = (tmp[rr, :] * dgel[gr, :]).astype(BF16)
            gpre[gr, :] = low
            vacc[3, :, :FW] = vacc[3, :, :FW] + fold(low.astype(F32))
            return carry

        lax.fori_loop(0, T // CH, chunk, 0)
        gm[r, :] = dot(cb, sc["wout"][...], NT).astype(BF16)

    for b in range(S):
        backward(pl.ds(b * T, T))
        if b == S // 2:
            tick(0)

    for k in range(NZ):
        tmp[:ZW, :] = dot(nrm[:, zcols(k)], gpre[...], TN)
        hand_out(1, k)
    tick(1)

    gk_a, gv_a, gq_a, mask_b = sc["gk"], sc["gv"], sc["gq"], sc["mask"]
    grads = sc["grads"]
    gk_a[...] = jnp.zeros_like(gk_a)
    gv_a[...] = jnp.zeros_like(gv_a)
    lane_q = lax.broadcasted_iota(jnp.int32, (1, LANES), 1)

    def attend(i):
        start = max(0, i * QB - window)
        nk = (i + 1) * QB - start
        qr = pl.ds(i * QB, QB)
        kr = pl.ds(start, nk)
        q_index = i * QB + lax.broadcasted_iota(jnp.int32, (QB, nk), 0)
        k_index = start + lax.broadcasted_iota(jnp.int32, (QB, nk), 1)
        allowed = (segc[qr, :] == segr[:, start : start + nk]) & (k_index <= q_index)
        mask_b[:, :nk] = jnp.where(allowed, 0.0, NEG_FILL)

        def head(h, carry):
            cols = pl.ds(pl.multiple_of(h // 2 * LANES, LANES), LANES)
            mine = (lane_q // HD) == (h % 2)
            qp = q_s[qr, cols]
            gp_rows = gm[qr, cols]
            kp = k_s[kr, cols]
            vp = v_s[kr, cols]
            zero = jnp.zeros((), BF16)
            s = dot(jnp.where(mine, qp, zero), kp, NT) + mask_b[:, :nk]
            e = jnp.exp(s - jnp.max(s, axis=-1, keepdims=True))
            p = e * (1.0 / jnp.sum(e, axis=-1, keepdims=True))
            p_low = p.astype(BF16)
            mixed = dot(p_low, vp, NN).astype(BF16)
            mix[qr, cols] = jnp.where(mine, mixed, mix[qr, cols])
            gp = dot(jnp.where(mine, gp_rows, zero), vp, NT)
            inner = jnp.sum(p * gp, axis=-1, keepdims=True)
            ds = (p * (gp - inner)).astype(BF16)
            gq_a[:, cols] = jnp.where(mine, dot(ds, kp, NN), gq_a[:, cols])
            gk_a[kr, cols] = gk_a[kr, cols] + jnp.where(mine, dot(ds, qp, TN), 0.0)
            gv_a[kr, cols] = gv_a[kr, cols] + jnp.where(mine, dot(p_low, gp_rows, TN), 0.0)
            return carry

        lax.fori_loop(0, HW // HD, head, 0)
        for t in range(HW // LANES):
            cols = slice(t * LANES, (t + 1) * LANES)
            grads[qr, cols] = turn(gq_a[:, cols] * scale, qr, -1.0).astype(BF16)

    done = 2
    for i in range(G // QB):
        attend(i)
        tick(done)
        done += 1
    for b in range(G // QB):
        r = pl.ds(b * QB, QB)
        for t in range(HW // LANES):
            cols = slice(t * LANES, (t + 1) * LANES)
            grads[r, HW + t * LANES : HW + (t + 1) * LANES] = turn(gk_a[r, cols], r, -1.0).astype(BF16)
            grads[r, 2 * HW + t * LANES : 2 * HW + (t + 1) * LANES] = gv_a[r, cols].astype(BF16)

    for k in range(NZ):
        tmp[:ZW, :HW] = dot(cot[:, zcols(k)], mix[...], TN)
        tmp[:ZW, HW : 4 * HW] = dot(nrm[:, zcols(k)], grads[...], TN)
        hand_out(2, k)

    keep, csend, crecv = sc["keep"], sc["csend"], sc["crecv"]
    ysend, yrecv = sc["ysend"], sc["yrecv"]
    css, crs, yss, yrs = sc["css"], sc["crs"], sc["yss"], sc["yrs"]

    def part_out(r):
        return dot(mix[r, :], sc["wout"][...], NN) + dot(hid[r, :], sc["wproj"][...], NN)

    def part_norm(r):
        total = dot(gpre[r, :], sc["win"][...], NT)
        for part in range(3):
            total = total + dot(
                grads[r, part * HW : (part + 1) * HW], sc["wqkv"][part], NT
            )
        return total

    def c_copy(a, d):
        return copy_to(csend.at[a, d], crecv.at[a, d], css.at[a, d], crs.at[a, d], sib)

    def y_copy(a, d):
        return copy_to(
            ysend.at[a, d - 1], yrecv.at[a, d - 1], yss.at[a, d - 1], yrs.at[a, d - 1], at_y((y + d) % NY)
        )

    order = list(range(1, NY)) + [0]

    def spread(a, fn):
        for d in order:
            csend[a, d] = fn(rows((y + d) % NY, 1 - c)).astype(BF16)
            c_copy(a, d).start()
            keep[a, d] = fn(rows((y + d) % NY, c)).astype(BF16)

    def pass_on(a):
        for d in order[:-1]:
            c_copy(a, d).wait()
            ysend[a, d - 1] = (keep[a, d].astype(F32) + crecv[a, d].astype(F32)).astype(BF16)
            y_copy(a, d).start()
        c_copy(a, 0).wait()

    def row_sum(a, r):
        total = keep[a, 0, r, :].astype(F32) + crecv[a, 0, r, :].astype(F32)
        for d in range(1, NY):
            total = total + yrecv[a, d - 1, r, :].astype(F32)
        return total

    spread(1, part_norm)
    pass_on(1)
    if done < 3 * NZ:
        tick(done)
        done += 1
    spread(0, part_out)
    pass_on(0)
    if done < 3 * NZ:
        tick(done)
        done += 1
    for d in range(1, NY):
        y_copy(1, d).wait()

    def finish_norm(r):
        _, xhat, inv = stats(r)
        gn = row_sum(1, r)
        cr_ = cot_own(r)
        e = gn * gain[...]
        dtok_o[r, :] = cr_ + inv * (
            e - jnp.mean(e, axis=-1, keepdims=True) - xhat * jnp.mean(e * xhat, axis=-1, keepdims=True)
        )
        vacc[0] = vacc[0] + fold(gn * xhat)
        vacc[1] = vacc[1] + fold(gn)
        vacc[2] = vacc[2] + fold(cr_)

    def cot_own(r):
        return cot[pl.ds(pl.multiple_of((y * 2 + c) * T + r.start, CH), CH), :].astype(F32)

    chunks(T, CH, finish_norm)

    v1, v1r, v2, v2r = sc["v1"], sc["v1r"], sc["v2"], sc["v2r"]
    v1[...] = jnp.zeros_like(v1)
    for row in range(4):
        v1[row : row + 1, :] = jnp.sum(vacc[row], axis=0, keepdims=True)

    def v1_copy(d):
        return copy_to(v1, v1r.at[d - 1], sc["v1s"].at[d - 1], sc["v1rs"].at[d - 1], ((dp + d) % DP, sp))

    def v2_copy(d):
        return copy_to(v2, v2r.at[d - 1], sc["v2s"].at[d - 1], sc["v2rs"].at[d - 1], (dp, (sp + d) % S))

    for d in range(1, DP):
        v1_copy(d).start()
    for d in range(1, NY):
        y_copy(0, d).wait()

    def finish_out(r):
        out_o[r, :] = (sc["tok"][r, :].astype(F32) + row_sum(0, r) + b_proj[...]).astype(BF16)

    chunks(T, CH, finish_out)
    while done < 3 * NZ - 2:
        tick(done)
        done += 1
    for d in range(1, DP):
        v1_copy(d).wait()
    total = v1[...]
    for d in range(1, DP):
        total = total + v1r[d - 1]
    v2[...] = total
    for d in range(1, S):
        v2_copy(d).start()
    while done <= 3 * NZ:
        tick(done)
        done += 1
    for d in range(1, S):
        v2_copy(d).wait()
    total = v2[...]
    for d in range(1, S):
        total = total + v2r[d - 1]
    vec_o[...] = total
    inb_o[pl.ds(sp, 1), :] = v2[3:4, :FW]
    for d in range(1, S):
        inb_o[pl.ds((sp + S - d) % S, 1), :] = v2r[d - 1, 3:4, :FW]
    for cp in sent:
        cp.wait_send()


def angles(positions):
    half_rot = ROT // 2
    frequency = 10000.0 ** (-2.0 * jnp.arange(half_rot, dtype=F32) / ROT)
    turned = positions.astype(F32)[:, None] * frequency[None, :]
    return jnp.cos(turned), jnp.sin(turned)


def positions_of(segment_row):
    before = jnp.sum((segment_row[None, :] < segment_row[:, None]).astype(jnp.int32), axis=1, dtype=jnp.int32)
    return jnp.arange(segment_row.shape[0], dtype=jnp.int32) - before


def turn_tables(segment_row):
    cosine, sine = angles(positions_of(segment_row))
    ones = jnp.ones((cosine.shape[0], HD - ROT), F32)
    one_c = jnp.concatenate([cosine, cosine, ones], axis=1)
    one_s = jnp.concatenate([-sine, sine, 0.0 * ones], axis=1)
    return jnp.tile(one_c, (1, LANES // HD)), jnp.tile(one_s, (1, LANES // HD))


def per_device(
    tokens,
    segment_ids,
    norm_gain,
    norm_bias,
    qkv_weight,
    out_weight,
    in_weight,
    in_bias,
    proj_weight,
    proj_bias,
    cotangent,
):
    T, D = tokens.shape
    G = segment_ids.shape[1]
    S, DP = lax.axis_size("sp"), lax.axis_size("dp")
    NX = math.isqrt(DP // 2)
    NZ = DP // NX
    NY = S // 2
    HW, FW = qkv_weight.shape[2] // S, in_weight.shape[1] // S
    DB, ZW = D // DP, D // NZ
    CW = FW
    nk = min(G, G // 2 + QB)
    seg = segment_ids[0]
    tab_c, tab_s = turn_tables(seg)

    vm = pltpu.VMEM
    dma = pltpu.SemaphoreType.DMA
    scratch = dict(
        tok=vm((T, D), BF16), nown=vm((T, D), BF16), nrm=vm((G, D), BF16), cot=vm((G, D), BF16),
        win=vm((D, FW), BF16), wproj=vm((FW, D), BF16), wqkv=vm((3, D, HW), BF16), wout=vm((HW, D), BF16),
        hid=vm((G, FW), BF16), dgel=vm((G, FW), F32), gpre=vm((G, FW), BF16),
        q=vm((G, HW), BF16), k=vm((G, HW), BF16), v=vm((G, HW), BF16), gm=vm((G, HW), BF16), mix=vm((G, HW), BF16),
        gk=vm((G, HW), F32), gv=vm((G, HW), F32), gq=vm((QB, HW), F32), mask=vm((QB, nk), F32),
        grads=vm((G, 3 * HW), BF16),
        tmp=vm((max(ZW, T), CW), F32),
        acc=vm((3, NZ, DB, CW), F32), xs=vm((3, NZ, NX - 1, DB, CW), BF16), xr=vm((3, NZ, NX - 1, DB, CW), BF16),
        zr=vm((3, NZ + 1, DB, CW), BF16),
        keep=vm((2, NY, T, D), BF16), csend=vm((2, NY, T, D), BF16), crecv=vm((2, NY, T, D), BF16),
        ysend=vm((2, NY - 1, T, D), BF16), yrecv=vm((2, NY - 1, T, D), BF16),
        vacc=vm((4, 8, D), F32), v1=vm((8, D), F32), v1r=vm((DP - 1, 8, D), F32),
        v2=vm((8, D), F32), v2r=vm((S - 1, 8, D), F32),
        ld_sem=dma((6,)), ns=dma((2 * NY - 1,)), nr=dma((2 * NY - 1,)),
        cs=dma((NZ, 2 * NY - 1)), cr=dma((NZ, 2 * NY - 1)),
        xss=dma((3, NZ, NX - 1)), xrs=dma((3, NZ, NX - 1)), zss=dma((3, NZ)), zrs=dma((3, NZ + 1)),
        css=dma((2, NY)), crs=dma((2, NY)), yss=dma((2, NY - 1)), yrs=dma((2, NY - 1)),
        v1s=dma((DP - 1,)), v1rs=dma((DP - 1,)), v2s=dma((S - 1,)), v2rs=dma((S - 1,)),
    )
    in_vmem = pl.BlockSpec(memory_space=pltpu.VMEM)
    anywhere = pl.BlockSpec(memory_space=pl.ANY)
    sizes = dict(
        n_in=14, n_out=7, scratch=tuple(scratch), T=T, D=D, G=G, S=S, DP=DP, NX=NX, NZ=NZ, NY=NY,
        HW=HW, FW=FW, DB=DB, ZW=ZW, CW=CW,
    )
    shape = jax.ShapeDtypeStruct
    out, d_tokens, sum_p, sum_i, sum_a, vec, inb = pl.pallas_call(
        functools.partial(block_kernel, sizes),
        out_shape=(
            shape((T, D), BF16), shape((T, D), F32), shape((DB, CW), F32), shape((DB, CW), F32),
            shape((DB, CW), F32), shape((8, D), F32), shape((S, FW), F32),
        ),
        in_specs=[anywhere] * 2 + [in_vmem] * 8 + [anywhere] * 4,
        out_specs=(in_vmem,) * 7,
        scratch_shapes=list(scratch.values()),
        compiler_params=pltpu.CompilerParams(
            collective_id=0, has_side_effects=True, vmem_limit_bytes=67043328
        ),
        name="block",
    )(
        tokens, cotangent, seg[:, None], seg[None, :], tab_c, tab_s, norm_gain[None, :], norm_bias[None, :],
        in_bias[None, :], proj_bias[None, :], qkv_weight, out_weight, in_weight, proj_weight,
    )
    g_qkv = jnp.stack([sum_a[:, (i + 1) * HW : (i + 2) * HW] for i in range(3)])
    return (
        out, d_tokens, vec[0], vec[1], g_qkv, sum_a[:, :HW].T, sum_i, inb.reshape(-1), sum_p.T, vec[2],
    )


def solution(mesh):
    placed = (
        P(("dp", "sp"), None), P("dp", None), P(), P(), P(), P(), P(), P(), P(), P(), P(("dp", "sp"), None),
    )
    return jax.shard_map(
        per_device,
        mesh=mesh,
        in_specs=placed,
        out_specs=(
            P(("dp", "sp"), None), P(("dp", "sp"), None), P(), P(), P(None, "dp", "sp"), P("sp", "dp"),
            P("dp", "sp"), P(), P("sp", "dp"), P(),
        ),
        check_vma=False,
    )
```

```python
import functools
import math

import jax
import jax.numpy as jnp
import numpy as np
from jax import lax
from jax.experimental import pallas as pl
from jax.experimental.pallas import tpu as pltpu
from jax.sharding import PartitionSpec as P

HD = 64
ROT = 32
LANES = 128
QB = 256
CH = 16
LN_CH = 64
STEP = 32

NEG_FILL = -1e30
F32 = jnp.float32
BF16 = jnp.bfloat16
MESH = pl.DeviceIdType.MESH

NN = (((1,), (0,)), ((), ()))
NT = (((1,), (1,)), ((), ()))
TN = (((0,), (0,)), ((), ()))

C0 = 0.7978845608028654
C1 = 0.044715


def dot(left, right, dims):
    return lax.dot_general(left, right, dims, preferred_element_type=F32)


def copy_to(src, dst, send, recv, target):
    return pltpu.make_async_remote_copy(
        src_ref=src, dst_ref=dst, send_sem=send, recv_sem=recv, device_id=target, device_id_type=MESH
    )


def chunks(count, step, fn):
    def one(i, carry):
        fn(pl.ds(pl.multiple_of(i * step, step), step))
        return carry

    lax.fori_loop(0, count // step, one, 0)


def block_kernel(sizes, *refs):
    n_in, n_out, names = sizes["n_in"], sizes["n_out"], sizes["scratch"]
    (tok_h, cot_h, segr, freq, gain, shift, b_in, b_proj, wqkv_h, wout_h, win_h, wproj_h) = refs[:n_in]
    (out_o, dtok_o, sum_p, sum_i, sum_a, vec_o, inb_o) = refs[n_in : n_in + n_out]
    sc = dict(zip(names, refs[n_in + n_out :]))
    T, D, G, S, DP = sizes["T"], sizes["D"], sizes["G"], sizes["S"], sizes["DP"]
    NX, NZ, NY = sizes["NX"], sizes["NZ"], sizes["NY"]
    HW, FW, DB, ZW, CW = sizes["HW"], sizes["FW"], sizes["DB"], sizes["ZW"], sizes["CW"]
    window = G // 2
    scale = 1.0 / math.sqrt(HD)

    nrm, cot, hid, dgel, gpre = sc["nrm"], sc["cot"], sc["hid"], sc["dgel"], sc["gpre"]
    q_s, k_s, v_s, gm, mix = sc["q"], sc["k"], sc["v"], sc["gm"], sc["mix"]
    tmp, acc, xs, xr, zr = sc["tmp"], sc["acc"], sc["xs"], sc["xr"], sc["zr"]
    outs = (sum_p, sum_i, sum_a)
    tab_c, tab_s, segc = sc["tab_c"], sc["tab_s"], sc["segc"]
    FZ = sizes["FZ"]
    FX = FW - FZ
    width = (FX, CW, CW)

    dp = lax.axis_index("dp")
    sp = lax.axis_index("sp")
    z, x, y, c = dp // NX, dp % NX, sp // 2, sp % 2
    sib = (dp, y * 2 + 1 - c)

    def at_y(y_):
        return (dp, y_ * 2 + c)

    def rows(y_, c_):
        return pl.ds(pl.multiple_of((y_ * 2 + c_) * T, T), T)

    own = rows(y, c)

    ld = sc["ld_sem"]
    load_tok = pltpu.make_async_copy(tok_h, sc["tok"], ld.at[0])
    load_cot = pltpu.make_async_copy(cot_h, cot.at[own, :], ld.at[1])
    fcols = pl.ds(pl.multiple_of(sp * FW, LANES), FW)
    hcols = pl.ds(pl.multiple_of(sp * HW, LANES), HW)
    load_in = pltpu.make_async_copy(win_h.at[:, fcols], sc["win"], ld.at[2])
    load_qkv = pltpu.make_async_copy(wqkv_h.at[:, :, hcols], sc["wqkv"], ld.at[3])
    load_proj = pltpu.make_async_copy(wproj_h.at[fcols, :], sc["wproj"], ld.at[4])
    load_out = pltpu.make_async_copy(wout_h.at[hcols, :], sc["wout"], ld.at[5])
    for load in (load_tok, load_cot, load_in, load_qkv, load_proj, load_out):
        load.start()

    barrier = pltpu.get_barrier_semaphore()
    for d in range(1, DP):
        pl.semaphore_signal(barrier, inc=1, device_id=((dp + d) % DP, sp), device_id_type=MESH)
    for d in range(1, S):
        pl.semaphore_signal(barrier, inc=1, device_id=(dp, (sp + d) % S), device_id_type=MESH)

    vacc = sc["vacc"]
    vacc[...] = jnp.zeros_like(vacc)

    def fold(value):
        return jnp.sum(value.reshape(CH // 8, 8, value.shape[-1]), axis=0)

    load_tok.wait()

    def norm_chunk(r):
        row = sc["tok"][r, :].astype(F32)
        mean = jnp.mean(row, axis=-1, keepdims=True)
        cent = row - mean
        var = jnp.mean(cent * cent, axis=-1, keepdims=True)
        inv = lax.rsqrt(var + 1e-05)
        sc["mean"][r, :] = jnp.broadcast_to(mean, (LN_CH, LANES))
        sc["inv"][r, :] = jnp.broadcast_to(inv, (LN_CH, LANES))
        nr_ = pl.ds(pl.multiple_of((y * 2 + c) * T + r.start, LN_CH), LN_CH)
        nrm[nr_, :] = (cent * inv * gain[...] + shift[...]).astype(BF16)

    def target(k):
        if k == NZ - 1:
            return z
        low = z < NZ // 2
        zz = jnp.where(low, z, NZ - 1 - z)
        v = NZ - 1 - k
        w = jnp.where(v <= zz, v - 1, v)
        return jnp.where(low, w, NZ - 1 - w)

    def zcols(k):
        return pl.ds(pl.multiple_of(target(k) * ZW, LANES), ZW)

    ns, nr, cs, cr = sc["ns"], sc["nr"], sc["cs"], sc["cr"]

    def send_rows(buf, view, ssem, rsem, slot, target_dev):
        cp = copy_to(buf.at[view], buf.at[view], ssem.at[slot], rsem.at[slot], target_dev)
        cp.start()
        return cp

    def got(buf, view, ssem, rsem, slot):
        copy_to(buf.at[view], buf.at[view], ssem.at[slot], rsem.at[slot], sib).wait_recv()

    sent = []

    def send_cot(k):
        for d in range(1, NY):
            sent.append(send_rows(cot, (own, zcols(k)), cs.at[k], cr.at[k], d, at_y((y + d) % NY)))
        sent.append(send_rows(cot, (own, zcols(k)), cs.at[k], cr.at[k], 0, sib))

    load_cot.wait()
    pl.semaphore_wait(barrier, DP - 1 + S - 1)
    send_cot(0)
    chunks(T, LN_CH, norm_chunk)
    for d in range(1, NY):
        sent.append(send_rows(nrm, (own, slice(None)), ns, nr, d, at_y((y + d) % NY)))
    sent.append(send_rows(nrm, (own, slice(None)), ns, nr, 0, sib))
    for k in range(1, NZ):
        send_cot(k)

    ids = segr[...].astype(F32)
    segc[...] = jnp.broadcast_to(ids, (LANES, G)).T
    lane_f = lax.broadcasted_iota(jnp.int32, (1, LANES), 1).astype(F32)
    starts = jnp.sum(jnp.where(segc[...] < lane_f, 1.0, 0.0), axis=0, keepdims=True)
    lane_h = lax.broadcasted_iota(jnp.int32, (1, LANES), 1) % HD

    def angle_chunk(r):
        hit = jnp.where(segc[r, :] == lane_f, starts, 0.0)
        begin = jnp.sum(hit, axis=1, keepdims=True)
        place = (lax.broadcasted_iota(jnp.int32, (T, 1), 0) + r.start).astype(F32) - begin
        angle = place * freq[...]
        tab_c[r, :] = jnp.where(lane_h < ROT, jnp.cos(angle), 1.0)
        sine = jnp.sin(angle)
        tab_s[r, :] = jnp.where(lane_h < ROT // 2, -sine, jnp.where(lane_h < ROT, sine, 0.0))

    chunks(G, T, angle_chunk)

    def relay_cot(k):
        for d in range(1, NY):
            view = (rows((y + NY - d) % NY, c), zcols(k))
            got(cot, view, cs.at[k], cr.at[k], d)
            sent.append(send_rows(cot, view, cs.at[k], cr.at[k], NY - 1 + d, sib))

    def wait_cot(k):
        got(cot, (rows(y, 1 - c), zcols(k)), cs.at[k], cr.at[k], 0)
        for d in range(1, NY):
            got(cot, (rows((y + NY - d) % NY, 1 - c), zcols(k)), cs.at[k], cr.at[k], NY - 1 + d)

    lane = lax.broadcasted_iota(jnp.int32, (T, LANES), 1)
    low_half = (lane % HD) < (ROT // 2)

    def turn(u, r, sign):
        partner = jnp.where(
            low_half[: u.shape[0]],
            pltpu.roll(u, LANES - ROT // 2, 1),
            pltpu.roll(u, ROT // 2, 1),
        )
        return u * tab_c[r, :] + sign * (partner * tab_s[r, :])

    bias_row = b_in[:, fcols]

    def forward(r):
        xb = nrm[r, :]
        tmp[:T, :] = dot(xb, sc["win"][...], NN)

        def gelu_chunk(i, carry):
            rr = pl.ds(pl.multiple_of(i * CH, CH), CH)
            gr = pl.ds(pl.multiple_of(r.start + i * CH, CH), CH)
            a = tmp[rr, :] + bias_row
            a2 = a * a
            th = jnp.tanh(C0 * (a + C1 * a2 * a))
            half = 0.5 * (1.0 + th)
            hid[gr, :] = (a * half).astype(BF16)
            dgel[gr, :] = half + 0.5 * a * (1.0 - th * th) * (C0 * (1.0 + 3.0 * C1 * a2))
            return carry

        lax.fori_loop(0, T // CH, gelu_chunk, 0)
        for part in range(3):
            u = dot(xb, sc["wqkv"][part], NN)
            for t in range(HW // LANES):
                cols = slice(t * LANES, (t + 1) * LANES)
                if part == 0:
                    q_s[r, cols] = turn(u[:, cols], r, 1.0).astype(BF16) * jnp.asarray(scale, BF16)
                elif part == 1:
                    k_s[r, cols] = turn(u[:, cols], r, 1.0).astype(BF16)
                else:
                    v_s[r, cols] = u[:, cols].astype(BF16)

    load_in.wait()
    load_qkv.wait()
    forward(own)
    got(nrm, (rows(y, 1 - c), slice(None)), ns, nr, 0)
    forward(rows(y, 1 - c))
    for d in range(1, NY):
        view = (rows((y + NY - d) % NY, c), slice(None))
        got(nrm, view, ns, nr, d)
        sent.append(send_rows(nrm, view, ns, nr, NY - 1 + d, sib))
        forward(view[0])
    relay_cot(0)
    for d in range(1, NY):
        view = (rows((y + NY - d) % NY, 1 - c), slice(None))
        got(nrm, view, ns, nr, NY - 1 + d)
        forward(view[0])
    relay_cot(1)

    xss, xrs, zss, zrs = sc["xss"], sc["xrs"], sc["zss"], sc["zrs"]

    def x_copy(g, k, d):
        cols = slice(0, width[g])
        return copy_to(
            xs.at[g, k, d - 1, :, cols], xr.at[g, k, d - 1, :, cols], xss.at[g, k, d - 1], xrs.at[g, k, d - 1],
            (z * NX + (x + d) % NX, sp),
        )

    def hand_out(g, k):
        cols = slice(0, width[g])
        for d in range(1, NX):

            def send_chunk(r):
                part = tmp[pl.ds(pl.multiple_of((x + d) % NX * DB + r.start, STEP), STEP), cols]
                xs[g, k, d - 1, r, cols] = part.astype(BF16)

            chunks(DB, STEP, send_chunk)
            x_copy(g, k, d).start()

        def keep_chunk(r):
            acc[g, k, r, cols] = tmp[pl.ds(pl.multiple_of(x * DB + r.start, STEP), STEP), cols]

        chunks(DB, STEP, keep_chunk)

    def z_slot(zt, nz, up):
        return jnp.where(up, zt, jnp.where(zt == nz, NZ, zt))

    def z_copy(g, k):
        zt = target(k)
        up = zt > z
        nz = jnp.where(up, z + 1, z - 1)
        slot = z_slot(zt, nz, up)
        cols = slice(0, width[g])
        return copy_to(
            xs.at[g, k, 0, :, cols], zr.at[g, slot, :, cols], zss.at[g, k], zrs.at[g, slot], (nz * NX + x, sp)
        )

    def z_got(g, slot):
        cols = slice(0, width[g])
        copy_to(
            xs.at[g, 0, 0, :, cols], zr.at[g, slot, :, cols], zss.at[g, 0], zrs.at[g, slot], sib
        ).wait_recv()

    def is_source(k):
        up = target(k) > z
        return jnp.where(up, z == 0, z == NZ - 1)

    def x_add(g, k):
        for d in range(1, NX):
            x_copy(g, k, d).wait()

        def add(r):
            cols = slice(0, width[g])
            total = acc[g, k, r, cols]
            for d in range(1, NX):
                total = total + xr[g, k, d - 1, r, cols].astype(F32)
            acc[g, k, r, cols] = total

        chunks(DB, STEP, add)

    def z_send(g, k):
        cols = slice(0, width[g])

        def low(r):
            xs[g, k, 0, r, cols] = acc[g, k, r, cols].astype(BF16)

        chunks(DB, STEP, low)
        z_copy(g, k).start()

    def z_first(g, k):
        @pl.when(is_source(k))
        def _():
            z_send(g, k)

    def z_next(g, k):
        @pl.when(jnp.logical_not(is_source(k)))
        def _():
            slot = target(k)
            z_got(g, slot)

            def add(r):
                cols = slice(0, width[g])
                acc[g, k, r, cols] = acc[g, k, r, cols] + zr[g, slot, r, cols].astype(F32)

            chunks(DB, STEP, add)
            z_send(g, k)

    def add_slot(g, slot):
        cols = slice(0, width[g])
        z_got(g, slot)

        def add(r):
            outs[g][r, cols] = outs[g][r, cols] + zr[g, slot, r, cols].astype(F32)

        chunks(DB, STEP, add)

    def z_last(g):
        cols = slice(0, width[g])

        def own_part(r):
            outs[g][r, cols] = acc[g, NZ - 1, r, cols]

        chunks(DB, STEP, own_part)
        if False:
            for d in range(1, NZ):
                add_slot(g, (z + d) % NZ)
        else:

            @pl.when(z > 0)
            def _():
                add_slot(g, z)

            @pl.when(z < NZ - 1)
            def _():
                add_slot(g, NZ)

        for j in range(NZ - 1):
            z_copy(g, j).wait_send()

    za, zb, zc = sc["za"], sc["zb"], sc["zc"]
    zas, zbs, xas, xbs = sc["zas"], sc["zbs"], sc["xas"], sc["xbs"]

    def f_copy(k):
        zt = target(k)
        up = zt > z
        nz = jnp.where(up, z + 1, z - 1)
        slot = z_slot(zt, nz, up)
        return copy_to(za.at[k], zb.at[slot], zas.at[k], zbs.at[slot], (nz * NX + x, sp))

    def f_got(slot):
        copy_to(za.at[0], zb.at[slot], zas.at[0], zbs.at[slot], sib).wait_recv()

    def f_out(k):
        zc[k] = tmp[:ZW, FX:]
        if k < NZ - 1:

            @pl.when(is_source(k))
            def _():
                za[k] = tmp[:ZW, FX:].astype(BF16)
                f_copy(k).start()

    def f_next(k):
        @pl.when(jnp.logical_not(is_source(k)))
        def _():
            slot = target(k)
            f_got(slot)
            za[k] = (zc[k] + zb[slot].astype(F32)).astype(BF16)
            f_copy(k).start()

    def fx_copy(d):
        return copy_to(
            sc["xa"].at[d - 1], sc["xb"].at[d - 1], xas.at[d - 1], xbs.at[d - 1], (z * NX + (x + d) % NX, sp)
        )

    def f_turn():
        k = NZ - 1

        @pl.when(z > 0)
        def _():
            f_got(z)
            zc[k] = zc[k] + zb[z].astype(F32)

        @pl.when(z < NZ - 1)
        def _():
            f_got(NZ)
            zc[k] = zc[k] + zb[NZ].astype(F32)

        for d in range(1, NX):
            part = zc[k, pl.ds(pl.multiple_of((x + d) % NX * DB, DB), DB), :]
            sc["xa"][d - 1] = part.astype(BF16)
            fx_copy(d).start()

    def f_last():
        total = zc[NZ - 1, pl.ds(pl.multiple_of(x * DB, DB), DB), :]
        for d in range(1, NX):
            fx_copy(d).wait()
            total = total + sc["xb"][d - 1].astype(F32)
        sum_p[:, FX:] = total
        for j in range(NZ - 1):
            f_copy(j).wait_send()

    def tick(n):
        g, k = n // NZ, n % NZ
        if n < 3 * NZ:
            x_add(g, k)
            if k < NZ - 1:
                z_first(g, k)
        if n > 0:
            g, k = (n - 1) // NZ, (n - 1) % NZ
            if k < NZ - 1:
                z_next(g, k)
            else:
                z_last(g)

    gk_a, gv_a, gq_a, mask_b = sc["gk"], sc["gv"], sc["gq"], sc["mask"]
    grads, lse_s, k_t, v_t = sc["grads"], sc["lse"], sc["kt"], sc["vt"]
    lane_q = lax.broadcasted_iota(jnp.int32, (1, LANES), 1)
    zero = jnp.zeros((), BF16)

    def set_mask(i):
        start = max(0, i * QB - window)
        nk = (i + 1) * QB - start
        q_index = i * QB + lax.broadcasted_iota(jnp.int32, (nk, QB), 1)
        k_index = start + lax.broadcasted_iota(jnp.int32, (nk, QB), 0)
        same = segc[start : start + nk, 0:1] == segr[:, i * QB : (i + 1) * QB].astype(F32)
        mask_b[:nk, :] = jnp.where(same & (k_index <= q_index), 0.0, NEG_FILL)
        return nk, slice(i * QB, (i + 1) * QB), slice(start, start + nk)

    def head_parts(h):
        cols = pl.ds(pl.multiple_of(h // 2 * LANES, LANES), LANES)
        return cols, (lane_q // HD) == (h % 2), pl.ds(pl.multiple_of(h * HD, HD), HD)

    def attend(i):
        nk, qr, kr = set_mask(i)

        def head(h, carry):
            cols, mine, hrows = head_parts(h)
            s = dot(k_s[kr, cols], jnp.where(mine, q_s[qr, cols], zero), NT) + mask_b[:nk, :]
            top = jnp.max(s, axis=0, keepdims=True)
            e = jnp.exp(s - top)
            total = jnp.sum(e, axis=0, keepdims=True)
            gq_a[hrows, :] = dot(v_t[hrows, kr], e.astype(BF16), NN) * (1.0 / total)
            lse_s[pl.ds(h, 1), qr] = top + jnp.log(total)
            return carry

        lax.fori_loop(0, HW // HD, head, 0)
        mix[qr, :] = gq_a[...].T.astype(BF16)

    def attend_back(i):
        nk, qr, kr = set_mask(i)

        def head(h, carry):
            cols, mine, hrows = head_parts(h)
            qp = jnp.where(mine, q_s[qr, cols], zero)
            gp_rows = jnp.where(mine, gm[qr, cols], zero)
            s = dot(k_s[kr, cols], qp, NT) + mask_b[:nk, :]
            p = jnp.exp(s - lse_s[pl.ds(h, 1), qr])
            gp = dot(v_s[kr, cols], gp_rows, NT)
            inner = jnp.sum(p * gp, axis=0, keepdims=True)
            ds = (p * (gp - inner)).astype(BF16)
            gq_a[hrows, :] = dot(k_t[hrows, kr], ds, NN)
            gk_a[kr, cols] = gk_a[kr, cols] + dot(ds, qp, NN)
            gv_a[kr, cols] = gv_a[kr, cols] + dot(p.astype(BF16), gp_rows, NN)
            return carry

        lax.fori_loop(0, HW // HD, head, 0, unroll=True)
        back = gq_a[...].T * scale
        for t in range(HW // LANES):
            cols = slice(t * LANES, (t + 1) * LANES)
            grads[qr, cols] = turn(back[:, cols], pl.ds(i * QB, QB), -1.0).astype(BF16)

    def key_grads():
        for b in range(G // QB):
            r = pl.ds(b * QB, QB)
            for t in range(HW // LANES):
                cols = slice(t * LANES, (t + 1) * LANES)
                grads[r, HW + t * LANES : HW + (t + 1) * LANES] = turn(gk_a[r, cols], r, -1.0).astype(BF16)
                grads[r, 2 * HW + t * LANES : 2 * HW + (t + 1) * LANES] = gv_a[r, cols].astype(BF16)

    keep, csend, crecv = sc["keep"], sc["csend"], sc["crecv"]
    ysend, yrecv = sc["ysend"], sc["yrecv"]
    css, crs, yss, yrs = sc["css"], sc["crs"], sc["yss"], sc["yrs"]

    def part_out(r):
        return dot(mix[r, :], sc["wout"][...], NN) + dot(hid[r, :], sc["wproj"][...], NN)

    early = FW == D

    def part_norm(r):
        total = dgel[r, :] if early else dot(gpre[r, :], sc["win"][...], NT)
        for part in range(3):
            total = total + dot(
                grads[r, part * HW : (part + 1) * HW], sc["wqkv"][part], NT
            )
        return total

    def c_copy(a, d):
        return copy_to(csend.at[d], crecv.at[a, d], css.at[a, d], crs.at[a, d], sib)

    def y_copy(a, d):
        return copy_to(
            ysend.at[a, d - 1], yrecv.at[a, d - 1], yss.at[a, d - 1], yrs.at[a, d - 1], at_y((y + d) % NY)
        )

    def spread(a, fn):
        for d in list(range(1, NY)) + [0]:
            csend[d] = fn(rows((y + d) % NY, 1 - c)).astype(BF16)
            c_copy(a, d).start()
            keep[a, d] = fn(rows((y + d) % NY, c)).astype(BF16)
            if d != 1 % NY:
                pass_on(a, (d if d else NY) - 1)
        c_copy(a, 0).wait()

    def pass_on(a, d):
        c_copy(a, d).wait()

        def add(r):
            ysend[a, d - 1, r, :] = (keep[a, d, r, :].astype(F32) + crecv[a, d, r, :].astype(F32)).astype(BF16)

        chunks(T, CH, add)
        y_copy(a, d).start()

    def row_sum(a, r):
        total = keep[a, 0, r, :].astype(F32) + crecv[a, 0, r, :].astype(F32)
        for d in range(1, NY):
            total = total + yrecv[a, d - 1, r, :].astype(F32)
        return total

    def backward(r):
        cb = cot[r, :]
        tmp[:T, :] = dot(cb, sc["wproj"][...], NT)

        def chunk(i, carry):
            rr = pl.ds(pl.multiple_of(i * CH, CH), CH)
            gr = pl.ds(pl.multiple_of(r.start + i * CH, CH), CH)
            low = (tmp[rr, :] * dgel[gr, :]).astype(BF16)
            gpre[gr, :] = low
            vacc[3, :, :FW] = vacc[3, :, :FW] + fold(low.astype(F32))
            return carry

        lax.fori_loop(0, T // CH, chunk, 0)
        gm[r, :] = dot(cb, sc["wout"][...], NT).astype(BF16)

    count = [0]

    def run_to(n):
        while count[0] < min(n, 3 * NZ + 1):
            tick(count[0])
            count[0] += 1

    k_t[...] = k_s[...].T
    v_t[...] = v_s[...].T

    blocks = G // QB
    steps = [functools.partial(f_next, k) for k in range(NZ - 1)] + [f_turn]
    made = [0, 0]

    def run_steps(upto):
        while made[0] < min(upto, len(steps)):
            steps[made[0]]()
            made[0] += 1

    def forward_to(upto):
        while made[1] < upto:
            attend(made[1])
            made[1] += 1

    for k in range(NZ):
        if k + 2 < NZ:
            relay_cot(k + 2)
        wait_cot(k)
        tmp[:ZW, :] = dot(cot[:, zcols(k)], hid[...], TN)
        hand_out(0, k)
        f_out(k)
        run_steps(k)
        forward_to((k + 1) * blocks // NZ)
    run_to(NZ // 4)

    load_proj.wait()
    load_out.wait()
    gk_a[...] = jnp.zeros_like(gk_a)
    gv_a[...] = jnp.zeros_like(gv_a)
    for b in range(S):
        backward(pl.ds(b * T, T))
        if b == 0:
            run_steps(NZ)
        if b == S // 2:
            run_to(NZ // 2)

    for k in range(NZ):
        tmp[:ZW, :] = dot(nrm[:, zcols(k)], gpre[...], TN)
        hand_out(1, k)
        if k == NZ // 2 - 1:
            run_to(3 * NZ // 4)
            spread(0, part_out)
    f_last()
    run_to(NZ)
    if early:
        for b in range(S):
            r = pl.ds(b * T, T)
            dgel[r, :] = dot(gpre[r, :], sc["win"][...], NT)

    v1, v1r, v2, v2r = sc["v1"], sc["v1r"], sc["v2"], sc["v2r"]

    def v1_copy(a, d):
        return copy_to(
            v1.at[a], v1r.at[a, d - 1], sc["v1s"].at[a, d - 1], sc["v1rs"].at[a, d - 1], ((dp + d) % DP, sp)
        )

    def v2_copy(a, d):
        return copy_to(
            v2.at[a], v2r.at[a, d - 1], sc["v2s"].at[a, d - 1], sc["v2rs"].at[a, d - 1], (dp, (sp + d) % S)
        )

    def vec_start(a):
        for row in range(2):
            v1[a, row : row + 1, :] = jnp.sum(vacc[2 * a + row], axis=0, keepdims=True)
        for d in range(1, DP):
            v1_copy(a, d).start()

    def vec_turn(a):
        total = v1[a]
        for d in range(1, DP):
            v1_copy(a, d).wait()
            total = total + v1r[a, d - 1]
        v2[a] = total
        for d in range(1, S):
            v2_copy(a, d).start()

    def vec_end(a):
        for d in range(1, S):
            v2_copy(a, d).wait()

    def vec_total(a):
        total = v2[a]
        for d in range(1, S):
            total = total + v2r[a, d - 1]
        return total

    def cot_own(r):
        return cot[pl.ds(pl.multiple_of((y * 2 + c) * T + r.start, CH), CH), :].astype(F32)

    def sum_cot(r):
        vacc[2] = vacc[2] + fold(cot_own(r))

    chunks(T, CH, sum_cot)
    vec_start(1)

    for i in range(blocks):
        attend_back(i)
        run_to(NZ + (i + 1) * NZ // (2 * blocks))
    key_grads()
    vec_turn(1)

    def last_group(k):
        tmp[:ZW, :HW] = dot(cot[:, zcols(k)], mix[...], TN)
        tmp[:ZW, HW : 4 * HW] = dot(nrm[:, zcols(k)], grads[...], TN)
        hand_out(2, k)

    spread(1, part_norm)
    for k in range(NZ):
        last_group(k)
    run_to(2 * NZ)
    for d in range(1, NY):
        y_copy(0, d).wait()

    def finish_out(r):
        out_o[r, :] = (sc["tok"][r, :].astype(F32) + row_sum(0, r) + b_proj[...]).astype(BF16)

    chunks(T, CH, finish_out)
    vec_end(1)
    for d in range(1, NY):
        y_copy(1, d).wait()

    def finish_norm(r):
        inv = sc["inv"][r, 0:1]
        xhat = (sc["tok"][r, :].astype(F32) - sc["mean"][r, 0:1]) * inv
        gn = row_sum(1, r)
        cr_ = cot_own(r)
        e = gn * gain[...]
        dtok_o[r, :] = cr_ + inv * (
            e - jnp.mean(e, axis=-1, keepdims=True) - xhat * jnp.mean(e * xhat, axis=-1, keepdims=True)
        )
        vacc[0] = vacc[0] + fold(gn * xhat)
        vacc[1] = vacc[1] + fold(gn)

    chunks(T, CH, finish_norm)

    vec_start(0)
    run_to(2 * NZ + NZ // 2)
    vec_turn(0)
    run_to(3 * NZ + 1)
    vec_end(0)
    vec_o[0:2, :] = vec_total(0)
    vec_o[2:4, :] = vec_total(1)
    inb_o[pl.ds(sp, 1), :] = v2[1, 1:2, :FW]
    for d in range(1, S):
        inb_o[pl.ds((sp + S - d) % S, 1), :] = v2r[1, d - 1, 1:2, :FW]
    for cp in sent:
        cp.wait_send()


def place_kernel(HW, FW, out, d_tokens, sum_p, sum_i, sum_a, vec, inb, *outs):
    out_o, dtok_o, gain_o, shift_o, qkv_o, outw_o, in_o, inb_o, proj_o, projb_o = outs
    out_o[...] = out[...]
    dtok_o[...] = d_tokens[...]
    gain_o[...] = vec[0:1, :]
    shift_o[...] = vec[1:2, :]
    projb_o[...] = vec[2:3, :]
    for i in range(3):
        qkv_o[i] = sum_a[:, (i + 1) * HW : (i + 2) * HW]
    outw_o[...] = sum_a[:, :HW].T
    in_o[...] = sum_i[...]
    proj_o[...] = sum_p[...].T
    for i in range(inb.shape[0]):
        inb_o[:, i * FW : (i + 1) * FW] = inb[i : i + 1, :]


def per_device(
    tokens,
    segment_ids,
    norm_gain,
    norm_bias,
    qkv_weight,
    out_weight,
    in_weight,
    in_bias,
    proj_weight,
    proj_bias,
    cotangent,
):
    T, D = tokens.shape
    G = segment_ids.shape[1]
    S, DP = lax.axis_size("sp"), lax.axis_size("dp")
    NX = math.isqrt(DP // 2)
    NZ = DP // NX
    NY = S // 2
    HW, FW = qkv_weight.shape[2] // S, in_weight.shape[1] // S
    DB, ZW = D // DP, D // NZ
    CW = FW
    nk = min(G, G // 2 + QB)
    FZ = FW // 4
    half = [10000.0 ** (-2.0 * f / ROT) for f in range(ROT // 2)]
    freq = jnp.asarray(np.tile(np.asarray(half, np.float32), LANES // len(half))[None, :])

    vm = pltpu.VMEM
    dma = pltpu.SemaphoreType.DMA
    scratch = dict(
        tok=vm((T, D), BF16), mean=vm((T, LANES), F32), inv=vm((T, LANES), F32),
        tab_c=vm((G, LANES), F32), tab_s=vm((G, LANES), F32), segc=vm((G, LANES), F32), nrm=vm((G, D), BF16), cot=vm((G, D), BF16),
        win=vm((D, FW), BF16), wproj=vm((FW, D), BF16), wqkv=vm((3, D, HW), BF16), wout=vm((HW, D), BF16),
        hid=vm((G, FW), BF16), dgel=vm((G, FW), F32), gpre=vm((G, FW), BF16),
        q=vm((G, HW), BF16), k=vm((G, HW), BF16), v=vm((G, HW), BF16), gm=vm((G, HW), BF16), mix=vm((G, HW), BF16),
        gk=vm((G, HW), F32), gv=vm((G, HW), F32), gq=vm((HW, QB), F32), mask=vm((nk, QB), F32),
        kt=vm((HW, G), BF16), vt=vm((HW, G), BF16),
        grads=vm((G, 3 * HW), BF16), lse=vm((8, G), F32),
        tmp=vm((max(ZW, T), CW), F32),
        acc=vm((3, NZ, DB, CW), F32), xs=vm((3, NZ, NX - 1, DB, CW), BF16), xr=vm((3, NZ, NX - 1, DB, CW), BF16),
        zr=vm((3, NZ + 1, DB, CW), BF16),
        za=vm((NZ, ZW, FZ), BF16), zb=vm((NZ + 1, ZW, FZ), BF16), zc=vm((NZ, ZW, FZ), F32),
        xa=vm((NX - 1, DB, FZ), BF16), xb=vm((NX - 1, DB, FZ), BF16),
        zas=dma((NZ,)), zbs=dma((NZ + 1,)), xas=dma((NX - 1,)), xbs=dma((NX - 1,)),
        keep=vm((2, NY, T, D), BF16), csend=vm((NY, T, D), BF16), crecv=vm((2, NY, T, D), BF16),
        ysend=vm((2, NY - 1, T, D), BF16), yrecv=vm((2, NY - 1, T, D), BF16),
        vacc=vm((4, 8, D), F32), v1=vm((2, 2, D), F32), v1r=vm((2, DP - 1, 2, D), F32),
        v2=vm((2, 2, D), F32), v2r=vm((2, S - 1, 2, D), F32),
        ld_sem=dma((6,)), ns=dma((2 * NY - 1,)), nr=dma((2 * NY - 1,)),
        cs=dma((NZ, 2 * NY - 1)), cr=dma((NZ, 2 * NY - 1)),
        xss=dma((3, NZ, NX - 1)), xrs=dma((3, NZ, NX - 1)), zss=dma((3, NZ)), zrs=dma((3, NZ + 1)),
        css=dma((2, NY)), crs=dma((2, NY)), yss=dma((2, NY - 1)), yrs=dma((2, NY - 1)),
        v1s=dma((2, DP - 1)), v1rs=dma((2, DP - 1)), v2s=dma((2, S - 1)), v2rs=dma((2, S - 1)),
    )
    in_vmem = pl.BlockSpec(memory_space=pltpu.VMEM)
    anywhere = pl.BlockSpec(memory_space=pl.ANY)
    sizes = dict(
        n_in=12, n_out=7, scratch=tuple(scratch), T=T, D=D, G=G, S=S, DP=DP, NX=NX, NZ=NZ, NY=NY,
        HW=HW, FW=FW, FZ=FZ, DB=DB, ZW=ZW, CW=CW,
    )
    shape = jax.ShapeDtypeStruct
    out, d_tokens, sum_p, sum_i, sum_a, vec, inb = pl.pallas_call(
        functools.partial(block_kernel, sizes),
        out_shape=(
            shape((T, D), BF16), shape((T, D), F32), shape((DB, CW), F32), shape((DB, CW), F32),
            shape((DB, CW), F32), shape((8, D), F32), shape((S, FW), F32),
        ),
        in_specs=[anywhere] * 2 + [in_vmem] * 6 + [anywhere] * 4,
        out_specs=(in_vmem,) * 7,
        scratch_shapes=list(scratch.values()),
        compiler_params=pltpu.CompilerParams(
            collective_id=0, has_side_effects=True, vmem_limit_bytes=67043328
        ),
        name="block",
    )(
        tokens, cotangent, segment_ids, freq, norm_gain[None, :], norm_bias[None, :],
        in_bias[None, :], proj_bias[None, :], qkv_weight, out_weight, in_weight, proj_weight,
    )
    parts = pl.pallas_call(
        functools.partial(place_kernel, HW, FW),
        out_shape=(
            shape((T, D), BF16), shape((T, D), F32), shape((1, D), F32), shape((1, D), F32),
            shape((3, DB, HW), F32), shape((HW, DB), F32), shape((DB, FW), F32), shape((1, S * FW), F32),
            shape((FW, DB), F32), shape((1, D), F32),
        ),
        in_specs=[in_vmem] * 7,
        out_specs=(in_vmem,) * 10,
        compiler_params=pltpu.CompilerParams(vmem_limit_bytes=67043328),
        name="place",
    )(out, d_tokens, sum_p, sum_i, sum_a, vec, inb)
    return tuple(p.reshape(-1) if p.shape[0] == 1 else p for p in parts)


def solution(mesh):
    placed = (
        P(("dp", "sp"), None), P("dp", None), P(), P(), P(), P(), P(), P(), P(), P(), P(("dp", "sp"), None),
    )
    return jax.shard_map(
        per_device,
        mesh=mesh,
        in_specs=placed,
        out_specs=(
            P(("dp", "sp"), None), P(("dp", "sp"), None), P(), P(), P(None, "dp", "sp"), P("sp", "dp"),
            P("dp", "sp"), P(), P("sp", "dp"), P(),
        ),
        check_vma=False,
    )
```

```python
import functools
import math

import jax
import jax.numpy as jnp
import numpy as np
from jax import lax
from jax.experimental import pallas as pl
from jax.experimental.pallas import tpu as pltpu
from jax.sharding import PartitionSpec as P

HD = 64
ROT = 32
LANES = 128
QB = 256
CH = 16
LN_CH = 64
STEP = 32

NEG_FILL = -1e30
F32 = jnp.float32
BF16 = jnp.bfloat16
MESH = pl.DeviceIdType.MESH

NN = (((1,), (0,)), ((), ()))
NT = (((1,), (1,)), ((), ()))
TN = (((0,), (0,)), ((), ()))

C0 = 0.7978845608028654
C1 = 0.044715


def dot(left, right, dims):
    return lax.dot_general(left, right, dims, preferred_element_type=F32)


def copy_to(src, dst, send, recv, target):
    return pltpu.make_async_remote_copy(
        src_ref=src, dst_ref=dst, send_sem=send, recv_sem=recv, device_id=target, device_id_type=MESH
    )


def chunks(count, step, fn):
    def one(i, carry):
        fn(pl.ds(pl.multiple_of(i * step, step), step))
        return carry

    lax.fori_loop(0, count // step, one, 0)


def block_kernel(sizes, *refs):
    n_in, n_out, names = sizes["n_in"], sizes["n_out"], sizes["scratch"]
    (tok_h, cot_h, segr, freq, gain, shift, b_in, b_proj, wqkv_h, wout_h, win_h, wproj_h) = refs[:n_in]
    (out_o, dtok_o, sum_p, sum_i, sum_a, vec_o, inb_o) = refs[n_in : n_in + n_out]
    sc = dict(zip(names, refs[n_in + n_out :]))
    T, D, G, S, DP = sizes["T"], sizes["D"], sizes["G"], sizes["S"], sizes["DP"]
    NX, NZ, NY = sizes["NX"], sizes["NZ"], sizes["NY"]
    HW, FW, DB, ZW, CW = sizes["HW"], sizes["FW"], sizes["DB"], sizes["ZW"], sizes["CW"]
    window = G // 2
    scale = 1.0 / math.sqrt(HD)

    nrm, cot, hid, dgel, gpre = sc["nrm"], sc["cot"], sc["hid"], sc["dgel"], sc["gpre"]
    q_s, k_s, v_s, gm, mix = sc["q"], sc["k"], sc["v"], sc["gm"], sc["mix"]
    tmp, acc, xs, xr, zr = sc["tmp"], sc["acc"], sc["xs"], sc["xr"], sc["zr"]
    outs = (sum_p, sum_i, sum_a)
    tab_c, tab_s, segc = sc["tab_c"], sc["tab_s"], sc["segc"]
    FZ = sizes["FZ"]
    FX = FW - FZ
    width = (FX, CW, CW)

    dp = lax.axis_index("dp")
    sp = lax.axis_index("sp")
    z, x, y, c = dp // NX, dp % NX, sp // 2, sp % 2
    sib = (dp, y * 2 + 1 - c)

    def at_y(y_):
        return (dp, y_ * 2 + c)

    def rows(y_, c_):
        return pl.ds(pl.multiple_of((y_ * 2 + c_) * T, T), T)

    own = rows(y, c)

    ld = sc["ld_sem"]
    load_tok = pltpu.make_async_copy(tok_h, sc["tok"], ld.at[0])
    load_cot = pltpu.make_async_copy(cot_h, cot.at[own, :], ld.at[1])
    fcols = pl.ds(pl.multiple_of(sp * FW, LANES), FW)
    hcols = pl.ds(pl.multiple_of(sp * HW, LANES), HW)
    load_in = pltpu.make_async_copy(win_h.at[:, fcols], sc["win"], ld.at[2])
    load_qkv = pltpu.make_async_copy(wqkv_h.at[:, :, hcols], sc["wqkv"], ld.at[3])
    load_proj = pltpu.make_async_copy(wproj_h.at[fcols, :], sc["wproj"], ld.at[4])
    load_out = pltpu.make_async_copy(wout_h.at[hcols, :], sc["wout"], ld.at[5])
    for load in (load_tok, load_cot, load_in, load_qkv, load_proj, load_out):
        load.start()

    barrier = pltpu.get_barrier_semaphore()
    for d in range(1, DP):
        pl.semaphore_signal(barrier, inc=1, device_id=((dp + d) % DP, sp), device_id_type=MESH)
    for d in range(1, S):
        pl.semaphore_signal(barrier, inc=1, device_id=(dp, (sp + d) % S), device_id_type=MESH)

    vacc = sc["vacc"]
    vacc[...] = jnp.zeros_like(vacc)

    def fold(value):
        return jnp.sum(value.reshape(CH // 8, 8, value.shape[-1]), axis=0)

    load_tok.wait()

    def norm_chunk(r):
        row = sc["tok"][r, :].astype(F32)
        mean = jnp.mean(row, axis=-1, keepdims=True)
        cent = row - mean
        var = jnp.mean(cent * cent, axis=-1, keepdims=True)
        inv = lax.rsqrt(var + 1e-05)
        sc["mean"][r, :] = jnp.broadcast_to(mean, (LN_CH, LANES))
        sc["inv"][r, :] = jnp.broadcast_to(inv, (LN_CH, LANES))
        nr_ = pl.ds(pl.multiple_of((y * 2 + c) * T + r.start, LN_CH), LN_CH)
        nrm[nr_, :] = (cent * inv * gain[...] + shift[...]).astype(BF16)

    def target(k):
        if k == NZ - 1:
            return z
        low = z < NZ // 2
        zz = jnp.where(low, z, NZ - 1 - z)
        v = NZ - 1 - k
        w = jnp.where(v <= zz, v - 1, v)
        return jnp.where(low, w, NZ - 1 - w)

    def zcols(k):
        return pl.ds(pl.multiple_of(target(k) * ZW, LANES), ZW)

    ns, nr, cs, cr = sc["ns"], sc["nr"], sc["cs"], sc["cr"]

    def send_rows(buf, view, ssem, rsem, slot, target_dev):
        cp = copy_to(buf.at[view], buf.at[view], ssem.at[slot], rsem.at[slot], target_dev)
        cp.start()
        return cp

    def got(buf, view, ssem, rsem, slot):
        copy_to(buf.at[view], buf.at[view], ssem.at[slot], rsem.at[slot], sib).wait_recv()

    sent = []

    def send_cot(k):
        for d in range(1, NY):
            sent.append(send_rows(cot, (own, zcols(k)), cs.at[k], cr.at[k], d, at_y((y + d) % NY)))
        sent.append(send_rows(cot, (own, zcols(k)), cs.at[k], cr.at[k], 0, sib))

    load_cot.wait()
    pl.semaphore_wait(barrier, DP - 1 + S - 1)
    send_cot(0)
    chunks(T, LN_CH, norm_chunk)
    for d in range(1, NY):
        sent.append(send_rows(nrm, (own, slice(None)), ns, nr, d, at_y((y + d) % NY)))
    sent.append(send_rows(nrm, (own, slice(None)), ns, nr, 0, sib))
    for k in range(1, NZ):
        send_cot(k)

    ids = segr[...].astype(F32)
    segc[...] = jnp.broadcast_to(ids, (LANES, G)).T
    lane_f = lax.broadcasted_iota(jnp.int32, (1, LANES), 1).astype(F32)
    starts = jnp.sum(jnp.where(segc[...] < lane_f, 1.0, 0.0), axis=0, keepdims=True)
    lane_h = lax.broadcasted_iota(jnp.int32, (1, LANES), 1) % HD

    def angle_chunk(r):
        hit = jnp.where(segc[r, :] == lane_f, starts, 0.0)
        begin = jnp.sum(hit, axis=1, keepdims=True)
        place = (lax.broadcasted_iota(jnp.int32, (T, 1), 0) + r.start).astype(F32) - begin
        angle = place * freq[...]
        tab_c[r, :] = jnp.where(lane_h < ROT, jnp.cos(angle), 1.0)
        sine = jnp.sin(angle)
        tab_s[r, :] = jnp.where(lane_h < ROT // 2, -sine, jnp.where(lane_h < ROT, sine, 0.0))

    chunks(G, T, angle_chunk)

    def relay_cot(k):
        for d in range(1, NY):
            view = (rows((y + NY - d) % NY, c), zcols(k))
            got(cot, view, cs.at[k], cr.at[k], d)
            sent.append(send_rows(cot, view, cs.at[k], cr.at[k], NY - 1 + d, sib))

    def wait_cot(k):
        got(cot, (rows(y, 1 - c), zcols(k)), cs.at[k], cr.at[k], 0)
        for d in range(1, NY):
            got(cot, (rows((y + NY - d) % NY, 1 - c), zcols(k)), cs.at[k], cr.at[k], NY - 1 + d)

    lane = lax.broadcasted_iota(jnp.int32, (T, LANES), 1)
    low_half = (lane % HD) < (ROT // 2)

    def turn(u, r, sign):
        partner = jnp.where(
            low_half[: u.shape[0]],
            pltpu.roll(u, LANES - ROT // 2, 1),
            pltpu.roll(u, ROT // 2, 1),
        )
        return u * tab_c[r, :] + sign * (partner * tab_s[r, :])

    bias_row = b_in[:, fcols]

    def forward(r):
        xb = nrm[r, :]
        tmp[:T, :] = dot(xb, sc["win"][...], NN)

        def gelu_chunk(i, carry):
            rr = pl.ds(pl.multiple_of(i * CH, CH), CH)
            gr = pl.ds(pl.multiple_of(r.start + i * CH, CH), CH)
            a = tmp[rr, :] + bias_row
            a2 = a * a
            th = jnp.tanh(C0 * (a + C1 * a2 * a))
            half = 0.5 * (1.0 + th)
            hid[gr, :] = (a * half).astype(BF16)
            dgel[gr, :] = half + 0.5 * a * (1.0 - th * th) * (C0 * (1.0 + 3.0 * C1 * a2))
            return carry

        lax.fori_loop(0, T // CH, gelu_chunk, 0)
        for part in range(3):
            u = dot(xb, sc["wqkv"][part], NN)
            for t in range(HW // LANES):
                cols = slice(t * LANES, (t + 1) * LANES)
                if part == 0:
                    q_s[r, cols] = turn(u[:, cols], r, 1.0).astype(BF16) * jnp.asarray(scale, BF16)
                elif part == 1:
                    k_s[r, cols] = turn(u[:, cols], r, 1.0).astype(BF16)
                else:
                    v_s[r, cols] = u[:, cols].astype(BF16)

    load_in.wait()
    load_qkv.wait()
    forward(own)
    got(nrm, (rows(y, 1 - c), slice(None)), ns, nr, 0)
    forward(rows(y, 1 - c))
    for d in range(1, NY):
        view = (rows((y + NY - d) % NY, c), slice(None))
        got(nrm, view, ns, nr, d)
        sent.append(send_rows(nrm, view, ns, nr, NY - 1 + d, sib))
        forward(view[0])
    relay_cot(0)
    for d in range(1, NY):
        view = (rows((y + NY - d) % NY, 1 - c), slice(None))
        got(nrm, view, ns, nr, NY - 1 + d)
        forward(view[0])
    relay_cot(1)

    xss, xrs, zss, zrs = sc["xss"], sc["xrs"], sc["zss"], sc["zrs"]

    def x_copy(g, k, d):
        cols = slice(0, width[g])
        return copy_to(
            xs.at[g, k, d - 1, :, cols], xr.at[g, k, d - 1, :, cols], xss.at[g, k, d - 1], xrs.at[g, k, d - 1],
            (z * NX + (x + d) % NX, sp),
        )

    def hand_out(g, k):
        cols = slice(0, width[g])
        for d in range(1, NX):

            def send_chunk(r):
                part = tmp[pl.ds(pl.multiple_of((x + d) % NX * DB + r.start, STEP), STEP), cols]
                xs[g, k, d - 1, r, cols] = part.astype(BF16)

            chunks(DB, STEP, send_chunk)
            if (g, k) != (2, NZ - 1):
                x_copy(g, k, d).start()

        def keep_chunk(r):
            acc[g, k, r, cols] = tmp[pl.ds(pl.multiple_of(x * DB + r.start, STEP), STEP), cols]

        chunks(DB, STEP, keep_chunk)

    def z_slot(zt, nz, up):
        return jnp.where(up, zt, jnp.where(zt == nz, NZ, zt))

    def z_copy(g, k):
        zt = target(k)
        up = zt > z
        nz = jnp.where(up, z + 1, z - 1)
        slot = z_slot(zt, nz, up)
        cols = slice(0, width[g])
        return copy_to(
            xs.at[g, k, 0, :, cols], zr.at[g, slot, :, cols], zss.at[g, k], zrs.at[g, slot], (nz * NX + x, sp)
        )

    def z_got(g, slot):
        cols = slice(0, width[g])
        copy_to(
            xs.at[g, 0, 0, :, cols], zr.at[g, slot, :, cols], zss.at[g, 0], zrs.at[g, slot], sib
        ).wait_recv()

    def is_source(k):
        up = target(k) > z
        return jnp.where(up, z == 0, z == NZ - 1)

    def x_add(g, k):
        for d in range(1, NX):
            x_copy(g, k, d).wait()

        def add(r):
            cols = slice(0, width[g])
            total = acc[g, k, r, cols]
            for d in range(1, NX):
                total = total + xr[g, k, d - 1, r, cols].astype(F32)
            acc[g, k, r, cols] = total

        chunks(DB, STEP, add)

    def z_send(g, k):
        cols = slice(0, width[g])

        def low(r):
            xs[g, k, 0, r, cols] = acc[g, k, r, cols].astype(BF16)

        chunks(DB, STEP, low)
        z_copy(g, k).start()

    def z_first(g, k):
        @pl.when(is_source(k))
        def _():
            z_send(g, k)

    def z_next(g, k):
        @pl.when(jnp.logical_not(is_source(k)))
        def _():
            slot = target(k)
            z_got(g, slot)

            def add(r):
                cols = slice(0, width[g])
                acc[g, k, r, cols] = acc[g, k, r, cols] + zr[g, slot, r, cols].astype(F32)

            chunks(DB, STEP, add)
            z_send(g, k)

    def add_slot(g, slot):
        cols = slice(0, width[g])
        z_got(g, slot)

        def add(r):
            outs[g][r, cols] = outs[g][r, cols] + zr[g, slot, r, cols].astype(F32)

        chunks(DB, STEP, add)

    def z_last(g):
        cols = slice(0, width[g])

        def own_part(r):
            outs[g][r, cols] = acc[g, NZ - 1, r, cols]

        chunks(DB, STEP, own_part)
        if False:
            for d in range(1, NZ):
                add_slot(g, (z + d) % NZ)
        else:

            @pl.when(z > 0)
            def _():
                add_slot(g, z)

            @pl.when(z < NZ - 1)
            def _():
                add_slot(g, NZ)

        for j in range(NZ - 1):
            z_copy(g, j).wait_send()

    za, zb, zc = sc["za"], sc["zb"], sc["zc"]
    zas, zbs, xas, xbs = sc["zas"], sc["zbs"], sc["xas"], sc["xbs"]

    def f_copy(k):
        zt = target(k)
        up = zt > z
        nz = jnp.where(up, z + 1, z - 1)
        slot = z_slot(zt, nz, up)
        return copy_to(za.at[k], zb.at[slot], zas.at[k], zbs.at[slot], (nz * NX + x, sp))

    def f_got(slot):
        copy_to(za.at[0], zb.at[slot], zas.at[0], zbs.at[slot], sib).wait_recv()

    def f_out(k):
        zc[k] = tmp[:ZW, FX:]
        if k < NZ - 1:

            @pl.when(is_source(k))
            def _():
                za[k] = tmp[:ZW, FX:].astype(BF16)
                f_copy(k).start()

    def f_next(k):
        @pl.when(jnp.logical_not(is_source(k)))
        def _():
            slot = target(k)
            f_got(slot)
            za[k] = (zc[k] + zb[slot].astype(F32)).astype(BF16)
            f_copy(k).start()

    def fx_copy(d):
        return copy_to(
            sc["xa"].at[d - 1], sc["xb"].at[d - 1], xas.at[d - 1], xbs.at[d - 1], (z * NX + (x + d) % NX, sp)
        )

    def f_turn():
        k = NZ - 1

        @pl.when(z > 0)
        def _():
            f_got(z)
            zc[k] = zc[k] + zb[z].astype(F32)

        @pl.when(z < NZ - 1)
        def _():
            f_got(NZ)
            zc[k] = zc[k] + zb[NZ].astype(F32)

        for d in range(1, NX):
            part = zc[k, pl.ds(pl.multiple_of((x + d) % NX * DB, DB), DB), :]
            sc["xa"][d - 1] = part.astype(BF16)
            fx_copy(d).start()

    def f_last():
        total = zc[NZ - 1, pl.ds(pl.multiple_of(x * DB, DB), DB), :]
        for d in range(1, NX):
            fx_copy(d).wait()
            total = total + sc["xb"][d - 1].astype(F32)
        sum_p[:, FX:] = total
        for j in range(NZ - 1):
            f_copy(j).wait_send()

    def x_tick(n):
        g, k = n // NZ, n % NZ
        x_add(g, k)
        if k < NZ - 1:
            z_first(g, k)

    def z_tick(n):
        g, k = n // NZ, n % NZ
        if k < NZ - 1:
            z_next(g, k)
        else:
            z_last(g)

    gk_a, gv_a, gq_a, mask_b = sc["gk"], sc["gv"], sc["gq"], sc["mask"]
    grads, lse_s, k_t, v_t = sc["grads"], sc["lse"], sc["kt"], sc["vt"]
    lane_q = lax.broadcasted_iota(jnp.int32, (1, LANES), 1)
    zero = jnp.zeros((), BF16)

    def set_mask(i):
        start = max(0, i * QB - window)
        nk = (i + 1) * QB - start
        q_index = i * QB + lax.broadcasted_iota(jnp.int32, (nk, QB), 1)
        k_index = start + lax.broadcasted_iota(jnp.int32, (nk, QB), 0)
        same = segc[start : start + nk, 0:1] == segr[:, i * QB : (i + 1) * QB].astype(F32)
        mask_b[:nk, :] = jnp.where(same & (k_index <= q_index), 0.0, NEG_FILL)
        return nk, slice(i * QB, (i + 1) * QB), slice(start, start + nk)

    def head_parts(h):
        cols = pl.ds(pl.multiple_of(h // 2 * LANES, LANES), LANES)
        return cols, (lane_q // HD) == (h % 2), pl.ds(pl.multiple_of(h * HD, HD), HD)

    def attend(i):
        nk, qr, kr = set_mask(i)

        def head(h, carry):
            cols, mine, hrows = head_parts(h)
            s = dot(k_s[kr, cols], jnp.where(mine, q_s[qr, cols], zero), NT) + mask_b[:nk, :]
            top = jnp.max(s, axis=0, keepdims=True)
            e = jnp.exp(s - top)
            total = jnp.sum(e, axis=0, keepdims=True)
            gq_a[hrows, :] = dot(v_t[hrows, kr], e.astype(BF16), NN) * (1.0 / total)
            lse_s[pl.ds(h, 1), qr] = top + jnp.log(total)
            return carry

        lax.fori_loop(0, HW // HD, head, 0)
        mix[qr, :] = gq_a[...].T.astype(BF16)

    def attend_back(i):
        nk, qr, kr = set_mask(i)

        def head(h, carry):
            cols, mine, hrows = head_parts(h)
            qp = jnp.where(mine, q_s[qr, cols], zero)
            gp_rows = jnp.where(mine, gm[qr, cols], zero)
            s = dot(k_s[kr, cols], qp, NT) + mask_b[:nk, :]
            p = jnp.exp(s - lse_s[pl.ds(h, 1), qr])
            gp = dot(v_s[kr, cols], gp_rows, NT)
            inner = jnp.sum(p * gp, axis=0, keepdims=True)
            ds = (p * (gp - inner)).astype(BF16)
            gq_a[hrows, :] = dot(k_t[hrows, kr], ds, NN)
            gk_a[kr, cols] = gk_a[kr, cols] + dot(ds, qp, NN)
            gv_a[kr, cols] = gv_a[kr, cols] + dot(p.astype(BF16), gp_rows, NN)
            return carry

        lax.fori_loop(0, HW // HD, head, 0, unroll=True)
        back = gq_a[...].T * scale
        for t in range(HW // LANES):
            cols = slice(t * LANES, (t + 1) * LANES)
            grads[qr, cols] = turn(back[:, cols], pl.ds(i * QB, QB), -1.0).astype(BF16)

    def key_grads():
        for b in range(G // QB):
            r = pl.ds(b * QB, QB)
            for t in range(HW // LANES):
                cols = slice(t * LANES, (t + 1) * LANES)
                grads[r, HW + t * LANES : HW + (t + 1) * LANES] = turn(gk_a[r, cols], r, -1.0).astype(BF16)
                grads[r, 2 * HW + t * LANES : 2 * HW + (t + 1) * LANES] = gv_a[r, cols].astype(BF16)

    keep, csend, crecv = sc["keep"], sc["csend"], sc["crecv"]
    ysend, yrecv = sc["ysend"], sc["yrecv"]
    css, crs, yss, yrs = sc["css"], sc["crs"], sc["yss"], sc["yrs"]

    def part_out(r):
        return dot(mix[r, :], sc["wout"][...], NN) + dot(hid[r, :], sc["wproj"][...], NN)

    def part_norm(r):
        total = dot(gpre[r, :], sc["win"][...], NT)
        for part in range(3):
            total = total + dot(
                grads[r, part * HW : (part + 1) * HW], sc["wqkv"][part], NT
            )
        return total

    def c_copy(a, d):
        return copy_to(csend.at[d], crecv.at[a, d], css.at[a, d], crs.at[a, d], sib)

    def y_copy(a, d):
        return copy_to(
            ysend.at[a, d - 1], yrecv.at[a, d - 1], yss.at[a, d - 1], yrs.at[a, d - 1], at_y((y + d) % NY)
        )

    def spread(a, fn):
        for d in list(range(1, NY)) + [0]:
            csend[d] = fn(rows((y + d) % NY, 1 - c)).astype(BF16)
            c_copy(a, d).start()
            keep[a, d] = fn(rows((y + d) % NY, c)).astype(BF16)
            if d != 1 % NY:
                pass_on(a, (d if d else NY) - 1)
        c_copy(a, 0).wait()

    def pass_on(a, d):
        c_copy(a, d).wait()

        def add(r):
            ysend[a, d - 1, r, :] = (keep[a, d, r, :].astype(F32) + crecv[a, d, r, :].astype(F32)).astype(BF16)

        chunks(T, CH, add)
        y_copy(a, d).start()

    def row_sum(a, r):
        total = keep[a, 0, r, :].astype(F32) + crecv[a, 0, r, :].astype(F32)
        for d in range(1, NY):
            total = total + yrecv[a, d - 1, r, :].astype(F32)
        return total

    def backward(r):
        cb = cot[r, :]
        tmp[:T, :] = dot(cb, sc["wproj"][...], NT)

        def chunk(i, carry):
            rr = pl.ds(pl.multiple_of(i * CH, CH), CH)
            gr = pl.ds(pl.multiple_of(r.start + i * CH, CH), CH)
            low = (tmp[rr, :] * dgel[gr, :]).astype(BF16)
            gpre[gr, :] = low
            vacc[3, :, :FW] = vacc[3, :, :FW] + fold(low.astype(F32))
            return carry

        lax.fori_loop(0, T // CH, chunk, 0)
        gm[r, :] = dot(cb, sc["wout"][...], NT).astype(BF16)

    count = [0, 0]

    def run_x(n):
        while count[0] < min(n, 3 * NZ):
            x_tick(count[0])
            count[0] += 1

    def run_z(n):
        while count[1] < min(n, 3 * NZ):
            z_tick(count[1])
            count[1] += 1

    def run_to(n):
        while count[0] < min(n, 3 * NZ):
            run_x(count[0] + 1)
            run_z(count[0] - 1)

    k_t[...] = k_s[...].T
    v_t[...] = v_s[...].T

    blocks = G // QB
    steps = [functools.partial(f_next, k) for k in range(NZ - 1)] + [f_turn]
    made = [0, 0]

    def run_steps(upto):
        while made[0] < min(upto, len(steps)):
            steps[made[0]]()
            made[0] += 1

    def forward_to(upto):
        while made[1] < upto:
            attend(made[1])
            made[1] += 1

    for k in range(NZ):
        if k + 2 < NZ:
            relay_cot(k + 2)
        wait_cot(k)
        tmp[:ZW, :] = dot(cot[:, zcols(k)], hid[...], TN)
        hand_out(0, k)
        f_out(k)
        run_steps(k)
        forward_to((k + 1) * blocks // NZ)
    run_to(NZ // 4)

    load_proj.wait()
    load_out.wait()
    gk_a[...] = jnp.zeros_like(gk_a)
    gv_a[...] = jnp.zeros_like(gv_a)
    for b in range(S):
        backward(pl.ds(b * T, T))
        if b == 0:
            run_steps(NZ)
        if b == S // 2:
            run_to(NZ // 2)

    for k in range(NZ):
        tmp[:ZW, :] = dot(nrm[:, zcols(k)], gpre[...], TN)
        hand_out(1, k)
        if k == NZ // 2 - 1:
            run_to(3 * NZ // 4)
    f_last()
    run_to(NZ)
    v1, v1r, v2, v2r = sc["v1"], sc["v1r"], sc["v2"], sc["v2r"]

    def v1_copy(a, d):
        return copy_to(
            v1.at[a], v1r.at[a, d - 1], sc["v1s"].at[a, d - 1], sc["v1rs"].at[a, d - 1], ((dp + d) % DP, sp)
        )

    def v2_copy(a, d):
        return copy_to(
            v2.at[a], v2r.at[a, d - 1], sc["v2s"].at[a, d - 1], sc["v2rs"].at[a, d - 1], (dp, (sp + d) % S)
        )

    def vec_start(a):
        for row in range(2):
            v1[a, row : row + 1, :] = jnp.sum(vacc[2 * a + row], axis=0, keepdims=True)
        for d in range(1, DP):
            v1_copy(a, d).start()

    def vec_turn(a):
        total = v1[a]
        for d in range(1, DP):
            v1_copy(a, d).wait()
            total = total + v1r[a, d - 1]
        v2[a] = total
        for d in range(1, S):
            v2_copy(a, d).start()

    def vec_end(a):
        for d in range(1, S):
            v2_copy(a, d).wait()

    def vec_total(a):
        total = v2[a]
        for d in range(1, S):
            total = total + v2r[a, d - 1]
        return total

    def cot_own(r):
        return cot[pl.ds(pl.multiple_of((y * 2 + c) * T + r.start, CH), CH), :].astype(F32)

    def sum_cot(r):
        vacc[2] = vacc[2] + fold(cot_own(r))

    chunks(T, CH, sum_cot)
    vec_start(1)

    for i in range(blocks):
        attend_back(i)
        run_x(NZ + (i + 1) * NZ // (2 * blocks))
    key_grads()

    def last_group(k):
        tmp[:ZW, :HW] = dot(cot[:, zcols(k)], mix[...], TN)
        tmp[:ZW, HW : 4 * HW] = dot(nrm[:, zcols(k)], grads[...], TN)
        hand_out(2, k)

    for k in range(NZ):
        last_group(k)
    spread(1, part_norm)
    run_to(2 * NZ - 1)
    spread(0, part_out)
    vec_turn(1)
    run_z(2 * NZ - 2)
    run_to(2 * NZ)

    for d in range(1, NY):
        y_copy(1, d).wait()

    def finish_norm(r):
        inv = sc["inv"][r, 0:1]
        xhat = (sc["tok"][r, :].astype(F32) - sc["mean"][r, 0:1]) * inv
        gn = row_sum(1, r)
        cr_ = cot_own(r)
        e = gn * gain[...]
        dtok_o[r, :] = cr_ + inv * (
            e - jnp.mean(e, axis=-1, keepdims=True) - xhat * jnp.mean(e * xhat, axis=-1, keepdims=True)
        )
        vacc[0] = vacc[0] + fold(gn * xhat)
        vacc[1] = vacc[1] + fold(gn)

    chunks(T, CH, finish_norm)

    vec_start(0)
    for d in range(1, NX):
        x_copy(2, NZ - 1, d).start()
    run_to(2 * NZ + NZ // 2)
    for d in range(1, NY):
        y_copy(0, d).wait()

    def finish_out(r):
        out_o[r, :] = (sc["tok"][r, :].astype(F32) + row_sum(0, r) + b_proj[...]).astype(BF16)

    chunks(T, CH, finish_out)
    run_to(3 * NZ - 1)
    run_z(3 * NZ - 1)
    run_to(3 * NZ)
    run_z(3 * NZ)
    vec_turn(0)
    vec_end(1)
    vec_end(0)
    vec_o[0:2, :] = vec_total(0)
    vec_o[2:4, :] = vec_total(1)
    inb_o[pl.ds(sp, 1), :] = v2[1, 1:2, :FW]
    for d in range(1, S):
        inb_o[pl.ds((sp + S - d) % S, 1), :] = v2r[1, d - 1, 1:2, :FW]
    for cp in sent:
        cp.wait_send()


def place_kernel(HW, FW, out, d_tokens, sum_p, sum_i, sum_a, vec, inb, *outs):
    out_o, dtok_o, gain_o, shift_o, qkv_o, outw_o, in_o, inb_o, proj_o, projb_o = outs
    out_o[...] = out[...]
    dtok_o[...] = d_tokens[...]
    gain_o[...] = vec[0:1, :]
    shift_o[...] = vec[1:2, :]
    projb_o[...] = vec[2:3, :]
    for i in range(3):
        qkv_o[i] = sum_a[:, (i + 1) * HW : (i + 2) * HW]
    outw_o[...] = sum_a[:, :HW].T
    in_o[...] = sum_i[...]
    proj_o[...] = sum_p[...].T
    for i in range(inb.shape[0]):
        inb_o[:, i * FW : (i + 1) * FW] = inb[i : i + 1, :]


def per_device(
    tokens,
    segment_ids,
    norm_gain,
    norm_bias,
    qkv_weight,
    out_weight,
    in_weight,
    in_bias,
    proj_weight,
    proj_bias,
    cotangent,
):
    T, D = tokens.shape
    G = segment_ids.shape[1]
    S, DP = lax.axis_size("sp"), lax.axis_size("dp")
    NX = math.isqrt(DP // 2)
    NZ = DP // NX
    NY = S // 2
    HW, FW = qkv_weight.shape[2] // S, in_weight.shape[1] // S
    DB, ZW = D // DP, D // NZ
    CW = FW
    nk = min(G, G // 2 + QB)
    FZ = FW // 4
    half = [10000.0 ** (-2.0 * f / ROT) for f in range(ROT // 2)]
    freq = jnp.asarray(np.tile(np.asarray(half, np.float32), LANES // len(half))[None, :])

    vm = pltpu.VMEM
    dma = pltpu.SemaphoreType.DMA
    scratch = dict(
        tok=vm((T, D), BF16), mean=vm((T, LANES), F32), inv=vm((T, LANES), F32),
        tab_c=vm((G, LANES), F32), tab_s=vm((G, LANES), F32), segc=vm((G, LANES), F32), nrm=vm((G, D), BF16), cot=vm((G, D), BF16),
        win=vm((D, FW), BF16), wproj=vm((FW, D), BF16), wqkv=vm((3, D, HW), BF16), wout=vm((HW, D), BF16),
        hid=vm((G, FW), BF16), dgel=vm((G, FW), F32), gpre=vm((G, FW), BF16),
        q=vm((G, HW), BF16), k=vm((G, HW), BF16), v=vm((G, HW), BF16), gm=vm((G, HW), BF16), mix=vm((G, HW), BF16),
        gk=vm((G, HW), F32), gv=vm((G, HW), F32), gq=vm((HW, QB), F32), mask=vm((nk, QB), F32),
        kt=vm((HW, G), BF16), vt=vm((HW, G), BF16),
        grads=vm((G, 3 * HW), BF16), lse=vm((8, G), F32),
        tmp=vm((max(ZW, T), CW), F32),
        acc=vm((3, NZ, DB, CW), F32), xs=vm((3, NZ, NX - 1, DB, CW), BF16), xr=vm((3, NZ, NX - 1, DB, CW), BF16),
        zr=vm((3, NZ + 1, DB, CW), BF16),
        za=vm((NZ, ZW, FZ), BF16), zb=vm((NZ + 1, ZW, FZ), BF16), zc=vm((NZ, ZW, FZ), F32),
        xa=vm((NX - 1, DB, FZ), BF16), xb=vm((NX - 1, DB, FZ), BF16),
        zas=dma((NZ,)), zbs=dma((NZ + 1,)), xas=dma((NX - 1,)), xbs=dma((NX - 1,)),
        keep=vm((2, NY, T, D), BF16), csend=vm((NY, T, D), BF16), crecv=vm((2, NY, T, D), BF16),
        ysend=vm((2, NY - 1, T, D), BF16), yrecv=vm((2, NY - 1, T, D), BF16),
        vacc=vm((4, 8, D), F32), v1=vm((2, 2, D), F32), v1r=vm((2, DP - 1, 2, D), F32),
        v2=vm((2, 2, D), F32), v2r=vm((2, S - 1, 2, D), F32),
        ld_sem=dma((6,)), ns=dma((2 * NY - 1,)), nr=dma((2 * NY - 1,)),
        cs=dma((NZ, 2 * NY - 1)), cr=dma((NZ, 2 * NY - 1)),
        xss=dma((3, NZ, NX - 1)), xrs=dma((3, NZ, NX - 1)), zss=dma((3, NZ)), zrs=dma((3, NZ + 1)),
        css=dma((2, NY)), crs=dma((2, NY)), yss=dma((2, NY - 1)), yrs=dma((2, NY - 1)),
        v1s=dma((2, DP - 1)), v1rs=dma((2, DP - 1)), v2s=dma((2, S - 1)), v2rs=dma((2, S - 1)),
    )
    in_vmem = pl.BlockSpec(memory_space=pltpu.VMEM)
    anywhere = pl.BlockSpec(memory_space=pl.ANY)
    sizes = dict(
        n_in=12, n_out=7, scratch=tuple(scratch), T=T, D=D, G=G, S=S, DP=DP, NX=NX, NZ=NZ, NY=NY,
        HW=HW, FW=FW, FZ=FZ, DB=DB, ZW=ZW, CW=CW,
    )
    shape = jax.ShapeDtypeStruct
    out, d_tokens, sum_p, sum_i, sum_a, vec, inb = pl.pallas_call(
        functools.partial(block_kernel, sizes),
        out_shape=(
            shape((T, D), BF16), shape((T, D), F32), shape((DB, CW), F32), shape((DB, CW), F32),
            shape((DB, CW), F32), shape((8, D), F32), shape((S, FW), F32),
        ),
        in_specs=[anywhere] * 2 + [in_vmem] * 6 + [anywhere] * 4,
        out_specs=(in_vmem,) * 7,
        scratch_shapes=list(scratch.values()),
        compiler_params=pltpu.CompilerParams(
            collective_id=0, has_side_effects=True, vmem_limit_bytes=67043328
        ),
        name="block",
    )(
        tokens, cotangent, segment_ids, freq, norm_gain[None, :], norm_bias[None, :],
        in_bias[None, :], proj_bias[None, :], qkv_weight, out_weight, in_weight, proj_weight,
    )
    parts = pl.pallas_call(
        functools.partial(place_kernel, HW, FW),
        out_shape=(
            shape((T, D), BF16), shape((T, D), F32), shape((1, D), F32), shape((1, D), F32),
            shape((3, DB, HW), F32), shape((HW, DB), F32), shape((DB, FW), F32), shape((1, S * FW), F32),
            shape((FW, DB), F32), shape((1, D), F32),
        ),
        in_specs=[in_vmem] * 7,
        out_specs=(in_vmem,) * 10,
        compiler_params=pltpu.CompilerParams(vmem_limit_bytes=67043328),
        name="place",
    )(out, d_tokens, sum_p, sum_i, sum_a, vec, inb)
    return tuple(p.reshape(-1) if p.shape[0] == 1 else p for p in parts)


def solution(mesh):
    placed = (
        P(("dp", "sp"), None), P("dp", None), P(), P(), P(), P(), P(), P(), P(), P(), P(("dp", "sp"), None),
    )
    return jax.shard_map(
        per_device,
        mesh=mesh,
        in_specs=placed,
        out_specs=(
            P(("dp", "sp"), None), P(("dp", "sp"), None), P(), P(), P(None, "dp", "sp"), P("sp", "dp"),
            P("dp", "sp"), P(), P("sp", "dp"), P(),
        ),
        check_vma=False,
    )
```

```python
import functools
import math

import jax
import jax.numpy as jnp
import numpy as np
from jax import lax
from jax.experimental import pallas as pl
from jax.experimental.pallas import tpu as pltpu
from jax.sharding import PartitionSpec as P

HD = 64
ROT = 32
LANES = 128
QB = 256
CH = 32
LN_CH = 64
STEP = 32

NEG_FILL = -1e30
F32 = jnp.float32
BF16 = jnp.bfloat16
MESH = pl.DeviceIdType.MESH

NN = (((1,), (0,)), ((), ()))
NT = (((1,), (1,)), ((), ()))
TN = (((0,), (0,)), ((), ()))

C0 = 0.7978845608028654
C1 = 0.044715


def dot(left, right, dims):
    return lax.dot_general(left, right, dims, preferred_element_type=F32)


def copy_to(src, dst, send, recv, target):
    return pltpu.make_async_remote_copy(
        src_ref=src, dst_ref=dst, send_sem=send, recv_sem=recv, device_id=target, device_id_type=MESH
    )


def chunks(count, step, fn):
    def one(i, carry):
        fn(pl.ds(pl.multiple_of(i * step, step), step))
        return carry

    lax.fori_loop(0, count // step, one, 0)


def block_kernel(sizes, *refs):
    n_in, n_out, names = sizes["n_in"], sizes["n_out"], sizes["scratch"]
    (tok_h, cot_h, segr, freq, gain, shift, b_in, b_proj, wqkv_h, wout_h, win_h, wproj_h) = refs[:n_in]
    (out_o, dtok_o, sum_p, sum_i, sum_a, vec_o, inb_o) = refs[n_in : n_in + n_out]
    sc = dict(zip(names, refs[n_in + n_out :]))
    T, D, G, S, DP = sizes["T"], sizes["D"], sizes["G"], sizes["S"], sizes["DP"]
    NX, NZ, NY = sizes["NX"], sizes["NZ"], sizes["NY"]
    HW, FW, DB, ZW, CW = sizes["HW"], sizes["FW"], sizes["DB"], sizes["ZW"], sizes["CW"]
    window = G // 2
    scale = 1.0 / math.sqrt(HD)

    nrm, cot, hid, dgel, gpre = sc["nrm"], sc["cot"], sc["hid"], sc["dgel"], sc["gpre"]
    q_s, k_s, v_s, gm, mix = sc["q"], sc["k"], sc["v"], sc["gm"], sc["mix"]
    tmp, acc, xs, xr, zr = sc["tmp"], sc["acc"], sc["xs"], sc["xr"], sc["zr"]
    outs = (sum_p, sum_i, sum_a)
    tab_c, tab_s, segc = sc["tab_c"], sc["tab_s"], sc["segc"]
    FZ = sizes["FZ"]
    FX = FW - FZ
    width = (FX, CW, CW)

    dp = lax.axis_index("dp")
    sp = lax.axis_index("sp")
    z, x, y, c = dp // NX, dp % NX, sp // 2, sp % 2
    sib = (dp, y * 2 + 1 - c)

    def at_y(y_):
        return (dp, y_ * 2 + c)

    def rows(y_, c_):
        return pl.ds(pl.multiple_of((y_ * 2 + c_) * T, T), T)

    own = rows(y, c)

    ld = sc["ld_sem"]
    load_tok = pltpu.make_async_copy(tok_h, sc["tok"], ld.at[0])
    load_cot = pltpu.make_async_copy(cot_h, cot.at[own, :], ld.at[1])
    fcols = pl.ds(pl.multiple_of(sp * FW, LANES), FW)
    hcols = pl.ds(pl.multiple_of(sp * HW, LANES), HW)
    load_in = pltpu.make_async_copy(win_h.at[:, fcols], sc["win"], ld.at[2])
    load_qkv = pltpu.make_async_copy(wqkv_h.at[:, :, hcols], sc["wqkv"], ld.at[3])
    load_proj = pltpu.make_async_copy(wproj_h.at[fcols, :], sc["wproj"], ld.at[4])
    load_out = pltpu.make_async_copy(wout_h.at[hcols, :], sc["wout"], ld.at[5])
    for load in (load_tok, load_cot, load_in, load_qkv, load_proj, load_out):
        load.start()

    barrier = pltpu.get_barrier_semaphore()
    for d in range(1, DP):
        pl.semaphore_signal(barrier, inc=1, device_id=((dp + d) % DP, sp), device_id_type=MESH)
    for d in range(1, S):
        pl.semaphore_signal(barrier, inc=1, device_id=(dp, (sp + d) % S), device_id_type=MESH)

    vacc = sc["vacc"]
    vacc[...] = jnp.zeros_like(vacc)

    def fold(value):
        return jnp.sum(value.reshape(CH // 8, 8, value.shape[-1]), axis=0)

    load_tok.wait()

    def norm_chunk(r):
        row = sc["tok"][r, :].astype(F32)
        mean = jnp.mean(row, axis=-1, keepdims=True)
        cent = row - mean
        var = jnp.mean(cent * cent, axis=-1, keepdims=True)
        inv = lax.rsqrt(var + 1e-05)
        sc["mean"][r, :] = jnp.broadcast_to(mean, (LN_CH, LANES))
        sc["inv"][r, :] = jnp.broadcast_to(inv, (LN_CH, LANES))
        nr_ = pl.ds(pl.multiple_of((y * 2 + c) * T + r.start, LN_CH), LN_CH)
        nrm[nr_, :] = (cent * inv * gain[...] + shift[...]).astype(BF16)

    def target(k):
        if k == NZ - 1:
            return z
        low = z < NZ // 2
        zz = jnp.where(low, z, NZ - 1 - z)
        v = NZ - 1 - k
        w = jnp.where(v <= zz, v - 1, v)
        return jnp.where(low, w, NZ - 1 - w)

    def zcols(k):
        return pl.ds(pl.multiple_of(target(k) * ZW, LANES), ZW)

    ns, nr, cs, cr = sc["ns"], sc["nr"], sc["cs"], sc["cr"]

    def send_rows(buf, view, ssem, rsem, slot, target_dev):
        cp = copy_to(buf.at[view], buf.at[view], ssem.at[slot], rsem.at[slot], target_dev)
        cp.start()
        return cp

    def got(buf, view, ssem, rsem, slot):
        copy_to(buf.at[view], buf.at[view], ssem.at[slot], rsem.at[slot], sib).wait_recv()

    sent = []

    def send_cot(k):
        for d in range(1, NY):
            sent.append(send_rows(cot, (own, zcols(k)), cs.at[k], cr.at[k], d, at_y((y + d) % NY)))
        sent.append(send_rows(cot, (own, zcols(k)), cs.at[k], cr.at[k], 0, sib))

    load_cot.wait()
    pl.semaphore_wait(barrier, DP - 1 + S - 1)
    send_cot(0)
    chunks(T, LN_CH, norm_chunk)
    for d in range(1, NY):
        sent.append(send_rows(nrm, (own, slice(None)), ns, nr, d, at_y((y + d) % NY)))
    sent.append(send_rows(nrm, (own, slice(None)), ns, nr, 0, sib))
    for k in range(1, NZ):
        send_cot(k)

    ids = segr[...].astype(F32)
    segc[...] = jnp.broadcast_to(ids, (LANES, G)).T
    lane_f = lax.broadcasted_iota(jnp.int32, (1, LANES), 1).astype(F32)
    starts = jnp.sum(jnp.where(segc[...] < lane_f, 1.0, 0.0), axis=0, keepdims=True)
    lane_h = lax.broadcasted_iota(jnp.int32, (1, LANES), 1) % HD

    def angle_chunk(r):
        hit = jnp.where(segc[r, :] == lane_f, starts, 0.0)
        begin = jnp.sum(hit, axis=1, keepdims=True)
        place = (lax.broadcasted_iota(jnp.int32, (T, 1), 0) + r.start).astype(F32) - begin
        angle = place * freq[...]
        tab_c[r, :] = jnp.where(lane_h < ROT, jnp.cos(angle), 1.0)
        sine = jnp.sin(angle)
        tab_s[r, :] = jnp.where(lane_h < ROT // 2, -sine, jnp.where(lane_h < ROT, sine, 0.0))

    chunks(G, T, angle_chunk)

    def relay_cot(k):
        for d in range(1, NY):
            view = (rows((y + NY - d) % NY, c), zcols(k))
            got(cot, view, cs.at[k], cr.at[k], d)
            sent.append(send_rows(cot, view, cs.at[k], cr.at[k], NY - 1 + d, sib))

    def wait_cot(k):
        got(cot, (rows(y, 1 - c), zcols(k)), cs.at[k], cr.at[k], 0)
        for d in range(1, NY):
            got(cot, (rows((y + NY - d) % NY, 1 - c), zcols(k)), cs.at[k], cr.at[k], NY - 1 + d)

    lane = lax.broadcasted_iota(jnp.int32, (T, LANES), 1)
    low_half = (lane % HD) < (ROT // 2)

    def turn(u, r, sign):
        partner = jnp.where(
            low_half[: u.shape[0]],
            pltpu.roll(u, LANES - ROT // 2, 1),
            pltpu.roll(u, ROT // 2, 1),
        )
        return u * tab_c[r, :] + sign * (partner * tab_s[r, :])

    bias_row = b_in[:, fcols]

    def forward(r):
        xb = nrm[r, :]
        tmp[:T, :] = dot(xb, sc["win"][...], NN)

        def gelu_chunk(i, carry):
            rr = pl.ds(pl.multiple_of(i * CH, CH), CH)
            gr = pl.ds(pl.multiple_of(r.start + i * CH, CH), CH)
            a = tmp[rr, :] + bias_row
            a2 = a * a
            th = jnp.tanh(C0 * (a + C1 * a2 * a))
            half = 0.5 * (1.0 + th)
            hid[gr, :] = (a * half).astype(BF16)
            dgel[gr, :] = half + 0.5 * a * (1.0 - th * th) * (C0 * (1.0 + 3.0 * C1 * a2))
            return carry

        lax.fori_loop(0, T // CH, gelu_chunk, 0)
        for part in range(3):
            u = dot(xb, sc["wqkv"][part], NN)
            for t in range(HW // LANES):
                cols = slice(t * LANES, (t + 1) * LANES)
                if part == 0:
                    q_s[r, cols] = turn(u[:, cols], r, 1.0).astype(BF16) * jnp.asarray(scale, BF16)
                elif part == 1:
                    k_s[r, cols] = turn(u[:, cols], r, 1.0).astype(BF16)
                else:
                    v_s[r, cols] = u[:, cols].astype(BF16)

    load_in.wait()
    load_qkv.wait()
    forward(own)
    got(nrm, (rows(y, 1 - c), slice(None)), ns, nr, 0)
    forward(rows(y, 1 - c))
    for d in range(1, NY):
        view = (rows((y + NY - d) % NY, c), slice(None))
        got(nrm, view, ns, nr, d)
        sent.append(send_rows(nrm, view, ns, nr, NY - 1 + d, sib))
        forward(view[0])
    relay_cot(0)
    for d in range(1, NY):
        view = (rows((y + NY - d) % NY, 1 - c), slice(None))
        got(nrm, view, ns, nr, NY - 1 + d)
        forward(view[0])
    relay_cot(1)

    xss, xrs, zss, zrs = sc["xss"], sc["xrs"], sc["zss"], sc["zrs"]

    def x_copy(g, k, d):
        cols = slice(0, width[g])
        return copy_to(
            xs.at[g, k, d - 1, :, cols], xr.at[g, k, d - 1, :, cols], xss.at[g, k, d - 1], xrs.at[g, k, d - 1],
            (z * NX + (x + d) % NX, sp),
        )

    def hand_out(g, k):
        cols = slice(0, width[g])
        for d in range(1, NX):

            def send_chunk(r):
                part = tmp[pl.ds(pl.multiple_of((x + d) % NX * DB + r.start, STEP), STEP), cols]
                xs[g, k, d - 1, r, cols] = part.astype(BF16)

            chunks(DB, STEP, send_chunk)
            if (g, k) != (2, NZ - 1):
                x_copy(g, k, d).start()

        def keep_chunk(r):
            acc[g, k, r, cols] = tmp[pl.ds(pl.multiple_of(x * DB + r.start, STEP), STEP), cols]

        chunks(DB, STEP, keep_chunk)

    def z_slot(zt, nz, up):
        return jnp.where(up, zt, jnp.where(zt == nz, NZ, zt))

    def z_copy(g, k):
        zt = target(k)
        up = zt > z
        nz = jnp.where(up, z + 1, z - 1)
        slot = z_slot(zt, nz, up)
        cols = slice(0, width[g])
        return copy_to(
            xs.at[g, k, 0, :, cols], zr.at[g, slot, :, cols], zss.at[g, k], zrs.at[g, slot], (nz * NX + x, sp)
        )

    def z_got(g, slot):
        cols = slice(0, width[g])
        copy_to(
            xs.at[g, 0, 0, :, cols], zr.at[g, slot, :, cols], zss.at[g, 0], zrs.at[g, slot], sib
        ).wait_recv()

    def is_source(k):
        up = target(k) > z
        return jnp.where(up, z == 0, z == NZ - 1)

    def x_add(g, k):
        for d in range(1, NX):
            x_copy(g, k, d).wait()

        def add(r):
            cols = slice(0, width[g])
            total = acc[g, k, r, cols]
            for d in range(1, NX):
                total = total + xr[g, k, d - 1, r, cols].astype(F32)
            acc[g, k, r, cols] = total

        chunks(DB, STEP, add)

    def z_send(g, k):
        cols = slice(0, width[g])

        def low(r):
            xs[g, k, 0, r, cols] = acc[g, k, r, cols].astype(BF16)

        chunks(DB, STEP, low)
        z_copy(g, k).start()

    def z_first(g, k):
        @pl.when(is_source(k))
        def _():
            z_send(g, k)

    def z_next(g, k):
        @pl.when(jnp.logical_not(is_source(k)))
        def _():
            slot = target(k)
            z_got(g, slot)

            def add(r):
                cols = slice(0, width[g])
                acc[g, k, r, cols] = acc[g, k, r, cols] + zr[g, slot, r, cols].astype(F32)

            chunks(DB, STEP, add)
            z_send(g, k)

    def add_slot(g, slot):
        cols = slice(0, width[g])
        z_got(g, slot)

        def add(r):
            outs[g][r, cols] = outs[g][r, cols] + zr[g, slot, r, cols].astype(F32)

        chunks(DB, STEP, add)

    def z_last(g):
        cols = slice(0, width[g])

        def own_part(r):
            outs[g][r, cols] = acc[g, NZ - 1, r, cols]

        chunks(DB, STEP, own_part)
        if False:
            for d in range(1, NZ):
                add_slot(g, (z + d) % NZ)
        else:

            @pl.when(z > 0)
            def _():
                add_slot(g, z)

            @pl.when(z < NZ - 1)
            def _():
                add_slot(g, NZ)

        for j in range(NZ - 1):
            z_copy(g, j).wait_send()

    za, zb, zc = sc["za"], sc["zb"], sc["zc"]
    zas, zbs, xas, xbs = sc["zas"], sc["zbs"], sc["xas"], sc["xbs"]

    def f_copy(k):
        zt = target(k)
        up = zt > z
        nz = jnp.where(up, z + 1, z - 1)
        slot = z_slot(zt, nz, up)
        return copy_to(za.at[k], zb.at[slot], zas.at[k], zbs.at[slot], (nz * NX + x, sp))

    def f_got(slot):
        copy_to(za.at[0], zb.at[slot], zas.at[0], zbs.at[slot], sib).wait_recv()

    def f_out(k):
        zc[k] = tmp[:ZW, FX:]
        if k < NZ - 1:

            @pl.when(is_source(k))
            def _():
                za[k] = tmp[:ZW, FX:].astype(BF16)
                f_copy(k).start()

    def f_next(k):
        @pl.when(jnp.logical_not(is_source(k)))
        def _():
            slot = target(k)
            f_got(slot)
            za[k] = (zc[k] + zb[slot].astype(F32)).astype(BF16)
            f_copy(k).start()

    def fx_copy(d):
        return copy_to(
            sc["xa"].at[d - 1], sc["xb"].at[d - 1], xas.at[d - 1], xbs.at[d - 1], (z * NX + (x + d) % NX, sp)
        )

    def f_turn():
        k = NZ - 1

        @pl.when(z > 0)
        def _():
            f_got(z)
            zc[k] = zc[k] + zb[z].astype(F32)

        @pl.when(z < NZ - 1)
        def _():
            f_got(NZ)
            zc[k] = zc[k] + zb[NZ].astype(F32)

        for d in range(1, NX):
            part = zc[k, pl.ds(pl.multiple_of((x + d) % NX * DB, DB), DB), :]
            sc["xa"][d - 1] = part.astype(BF16)
            fx_copy(d).start()

    def f_last():
        total = zc[NZ - 1, pl.ds(pl.multiple_of(x * DB, DB), DB), :]
        for d in range(1, NX):
            fx_copy(d).wait()
            total = total + sc["xb"][d - 1].astype(F32)
        sum_p[:, FX:] = total
        for j in range(NZ - 1):
            f_copy(j).wait_send()

    def x_tick(n):
        g, k = n // NZ, n % NZ
        x_add(g, k)
        if k < NZ - 1:
            z_first(g, k)

    def z_tick(n):
        g, k = n // NZ, n % NZ
        if k < NZ - 1:
            z_next(g, k)
        else:
            z_last(g)

    gk_a, gv_a, gq_a, mask_b = sc["gk"], sc["gv"], sc["gq"], sc["mask"]
    grads, lse_s, k_t, v_t = sc["grads"], sc["lse"], sc["kt"], sc["vt"]
    lane_q = lax.broadcasted_iota(jnp.int32, (1, LANES), 1)
    zero = jnp.zeros((), BF16)

    def set_mask(i):
        start = max(0, i * QB - window)
        nk = (i + 1) * QB - start
        q_index = i * QB + lax.broadcasted_iota(jnp.int32, (nk, QB), 1)
        k_index = start + lax.broadcasted_iota(jnp.int32, (nk, QB), 0)
        same = segc[start : start + nk, 0:1] == segr[:, i * QB : (i + 1) * QB].astype(F32)
        mask_b[:nk, :] = jnp.where(same & (k_index <= q_index), 0.0, NEG_FILL)
        return nk, slice(i * QB, (i + 1) * QB), slice(start, start + nk)

    def head_parts(h):
        cols = pl.ds(pl.multiple_of(h // 2 * LANES, LANES), LANES)
        return cols, (lane_q // HD) == (h % 2), pl.ds(pl.multiple_of(h * HD, HD), HD)

    def attend(i):
        nk, qr, kr = set_mask(i)

        def head(h, carry):
            cols, mine, hrows = head_parts(h)
            s = dot(k_s[kr, cols], jnp.where(mine, q_s[qr, cols], zero), NT) + mask_b[:nk, :]
            top = jnp.max(s, axis=0, keepdims=True)
            e = jnp.exp(s - top)
            total = jnp.sum(e, axis=0, keepdims=True)
            gq_a[hrows, :] = dot(v_t[hrows, kr], e.astype(BF16), NN) * (1.0 / total)
            lse_s[pl.ds(h, 1), qr] = top + jnp.log(total)
            return carry

        lax.fori_loop(0, HW // HD, head, 0)
        mix[qr, :] = gq_a[...].T.astype(BF16)

    def attend_back(i):
        nk, qr, kr = set_mask(i)

        def head(h, carry):
            cols, mine, hrows = head_parts(h)
            qp = jnp.where(mine, q_s[qr, cols], zero)
            gp_rows = jnp.where(mine, gm[qr, cols], zero)
            s = dot(k_s[kr, cols], qp, NT) + mask_b[:nk, :]
            p = jnp.exp(s - lse_s[pl.ds(h, 1), qr])
            gp = dot(v_s[kr, cols], gp_rows, NT)
            inner = jnp.sum(p * gp, axis=0, keepdims=True)
            ds = (p * (gp - inner)).astype(BF16)
            gq_a[hrows, :] = dot(k_t[hrows, kr], ds, NN)
            gk_a[kr, cols] = gk_a[kr, cols] + dot(ds, qp, NN)
            gv_a[kr, cols] = gv_a[kr, cols] + dot(p.astype(BF16), gp_rows, NN)
            return carry

        lax.fori_loop(0, HW // HD, head, 0, unroll=True)
        back = gq_a[...].T * scale
        for t in range(HW // LANES):
            cols = slice(t * LANES, (t + 1) * LANES)
            grads[qr, cols] = turn(back[:, cols], pl.ds(i * QB, QB), -1.0).astype(BF16)

    def key_grads():
        for b in range(G // QB):
            r = pl.ds(b * QB, QB)
            for t in range(HW // LANES):
                cols = slice(t * LANES, (t + 1) * LANES)
                grads[r, HW + t * LANES : HW + (t + 1) * LANES] = turn(gk_a[r, cols], r, -1.0).astype(BF16)
                grads[r, 2 * HW + t * LANES : 2 * HW + (t + 1) * LANES] = gv_a[r, cols].astype(BF16)

    keep, csend, crecv = sc["keep"], sc["csend"], sc["crecv"]
    ysend, yrecv = sc["ysend"], sc["yrecv"]
    css, crs, yss, yrs = sc["css"], sc["crs"], sc["yss"], sc["yrs"]

    def part_out(r):
        return dot(mix[r, :], sc["wout"][...], NN) + dot(hid[r, :], sc["wproj"][...], NN)

    def part_norm(r):
        total = dot(gpre[r, :], sc["win"][...], NT)
        for part in range(3):
            total = total + dot(
                grads[r, part * HW : (part + 1) * HW], sc["wqkv"][part], NT
            )
        return total

    def c_copy(a, d):
        return copy_to(csend.at[d], crecv.at[a, d], css.at[a, d], crs.at[a, d], sib)

    def y_copy(a, d):
        return copy_to(
            ysend.at[a, d - 1], yrecv.at[a, d - 1], yss.at[a, d - 1], yrs.at[a, d - 1], at_y((y + d) % NY)
        )

    def spread(a, fn):
        for d in list(range(1, NY)) + [0]:
            csend[d] = fn(rows((y + d) % NY, 1 - c)).astype(BF16)
            c_copy(a, d).start()
            keep[a, d] = fn(rows((y + d) % NY, c)).astype(BF16)
            if d != 1 % NY:
                pass_on(a, (d if d else NY) - 1)
        c_copy(a, 0).wait()

    def pass_on(a, d):
        c_copy(a, d).wait()

        def add(r):
            ysend[a, d - 1, r, :] = (keep[a, d, r, :].astype(F32) + crecv[a, d, r, :].astype(F32)).astype(BF16)

        chunks(T, CH, add)
        y_copy(a, d).start()

    def row_sum(a, r):
        total = keep[a, 0, r, :].astype(F32) + crecv[a, 0, r, :].astype(F32)
        for d in range(1, NY):
            total = total + yrecv[a, d - 1, r, :].astype(F32)
        return total

    def backward(r):
        cb = cot[r, :]
        tmp[:T, :] = dot(cb, sc["wproj"][...], NT)

        def chunk(i, carry):
            rr = pl.ds(pl.multiple_of(i * CH, CH), CH)
            gr = pl.ds(pl.multiple_of(r.start + i * CH, CH), CH)
            low = (tmp[rr, :] * dgel[gr, :]).astype(BF16)
            gpre[gr, :] = low
            vacc[3, :, :FW] = vacc[3, :, :FW] + fold(low.astype(F32))
            return carry

        lax.fori_loop(0, T // CH, chunk, 0)
        gm[r, :] = dot(cb, sc["wout"][...], NT).astype(BF16)

    count = [0, 0]

    def run_x(n):
        while count[0] < min(n, 3 * NZ):
            x_tick(count[0])
            count[0] += 1

    def run_z(n):
        while count[1] < min(n, 3 * NZ):
            z_tick(count[1])
            count[1] += 1

    def run_to(n):
        while count[0] < min(n, 3 * NZ):
            run_x(count[0] + 1)
            run_z(count[0] - 1)

    k_t[...] = k_s[...].T
    v_t[...] = v_s[...].T

    blocks = G // QB
    steps = [functools.partial(f_next, k) for k in range(NZ - 1)] + [f_turn]
    made = [0, 0]

    def run_steps(upto):
        while made[0] < min(upto, len(steps)):
            steps[made[0]]()
            made[0] += 1

    def forward_to(upto):
        while made[1] < upto:
            attend(made[1])
            made[1] += 1

    for k in range(NZ):
        if k + 2 < NZ:
            relay_cot(k + 2)
        wait_cot(k)
        tmp[:ZW, :] = dot(cot[:, zcols(k)], hid[...], TN)
        hand_out(0, k)
        f_out(k)
        run_steps(k)
        forward_to((k + 1) * blocks // NZ)
    run_to(NZ // 4)

    load_proj.wait()
    load_out.wait()
    gk_a[...] = jnp.zeros_like(gk_a)
    gv_a[...] = jnp.zeros_like(gv_a)
    for b in range(S):
        backward(pl.ds(b * T, T))
        if b == 0:
            run_steps(NZ)
        if b == S // 2:
            run_to(NZ // 2)

    for k in range(NZ):
        tmp[:ZW, :] = dot(nrm[:, zcols(k)], gpre[...], TN)
        hand_out(1, k)
        if k == NZ // 2 - 1:
            run_to(3 * NZ // 4)
    f_last()
    run_to(NZ)
    v1, v1r, v2, v2r = sc["v1"], sc["v1r"], sc["v2"], sc["v2r"]

    def v1_copy(a, d):
        return copy_to(
            v1.at[a], v1r.at[a, d - 1], sc["v1s"].at[a, d - 1], sc["v1rs"].at[a, d - 1], ((dp + d) % DP, sp)
        )

    def v2_copy(a, d):
        return copy_to(
            v2.at[a], v2r.at[a, d - 1], sc["v2s"].at[a, d - 1], sc["v2rs"].at[a, d - 1], (dp, (sp + d) % S)
        )

    def vec_start(a):
        for row in range(2):
            v1[a, row : row + 1, :] = jnp.sum(vacc[2 * a + row], axis=0, keepdims=True)
        for d in range(1, DP):
            v1_copy(a, d).start()

    def vec_turn(a):
        total = v1[a]
        for d in range(1, DP):
            v1_copy(a, d).wait()
            total = total + v1r[a, d - 1]
        v2[a] = total
        for d in range(1, S):
            v2_copy(a, d).start()

    def vec_end(a):
        for d in range(1, S):
            v2_copy(a, d).wait()

    def vec_total(a):
        total = v2[a]
        for d in range(1, S):
            total = total + v2r[a, d - 1]
        return total

    def cot_own(r):
        return cot[pl.ds(pl.multiple_of((y * 2 + c) * T + r.start, CH), CH), :].astype(F32)

    def sum_cot(r):
        vacc[2] = vacc[2] + fold(cot_own(r))

    chunks(T, CH, sum_cot)
    vec_start(1)

    for i in range(blocks):
        attend_back(i)
        run_x(NZ + (i + 1) * NZ // (2 * blocks))
    key_grads()

    def last_group(k):
        tmp[:ZW, :HW] = dot(cot[:, zcols(k)], mix[...], TN)
        tmp[:ZW, HW : 4 * HW] = dot(nrm[:, zcols(k)], grads[...], TN)
        hand_out(2, k)

    for k in range(NZ):
        last_group(k)
    spread(1, part_norm)
    run_to(2 * NZ - 1)
    spread(0, part_out)
    vec_turn(1)
    run_z(2 * NZ - 2)
    run_to(2 * NZ)

    for d in range(1, NY):
        y_copy(1, d).wait()

    def finish_norm(r):
        inv = sc["inv"][r, 0:1]
        xhat = (sc["tok"][r, :].astype(F32) - sc["mean"][r, 0:1]) * inv
        gn = row_sum(1, r)
        cr_ = cot_own(r)
        e = gn * gain[...]
        dtok_o[r, :] = cr_ + inv * (
            e - jnp.mean(e, axis=-1, keepdims=True) - xhat * jnp.mean(e * xhat, axis=-1, keepdims=True)
        )
        vacc[0] = vacc[0] + fold(gn * xhat)
        vacc[1] = vacc[1] + fold(gn)

    chunks(T, CH, finish_norm)

    vec_start(0)
    for d in range(1, NX):
        x_copy(2, NZ - 1, d).start()
    run_to(2 * NZ + NZ // 2)
    for d in range(1, NY):
        y_copy(0, d).wait()

    def finish_out(r):
        out_o[r, :] = (sc["tok"][r, :].astype(F32) + row_sum(0, r) + b_proj[...]).astype(BF16)

    chunks(T, CH, finish_out)
    run_to(3 * NZ - 1)
    run_z(3 * NZ - 1)
    run_to(3 * NZ)
    run_z(3 * NZ)
    vec_turn(0)
    vec_end(1)
    vec_end(0)
    vec_o[0:2, :] = vec_total(0)
    vec_o[2:4, :] = vec_total(1)
    inb_o[pl.ds(sp, 1), :] = v2[1, 1:2, :FW]
    for d in range(1, S):
        inb_o[pl.ds((sp + S - d) % S, 1), :] = v2r[1, d - 1, 1:2, :FW]
    for cp in sent:
        cp.wait_send()


def place_kernel(HW, FW, out, d_tokens, sum_p, sum_i, sum_a, vec, inb, *outs):
    out_o, dtok_o, gain_o, shift_o, qkv_o, outw_o, in_o, inb_o, proj_o, projb_o = outs
    out_o[...] = out[...]
    dtok_o[...] = d_tokens[...]
    gain_o[...] = vec[0:1, :]
    shift_o[...] = vec[1:2, :]
    projb_o[...] = vec[2:3, :]
    for i in range(3):
        qkv_o[i] = sum_a[:, (i + 1) * HW : (i + 2) * HW]
    outw_o[...] = sum_a[:, :HW].T
    in_o[...] = sum_i[...]
    proj_o[...] = sum_p[...].T
    for i in range(inb.shape[0]):
        inb_o[:, i * FW : (i + 1) * FW] = inb[i : i + 1, :]


def per_device(
    tokens,
    segment_ids,
    norm_gain,
    norm_bias,
    qkv_weight,
    out_weight,
    in_weight,
    in_bias,
    proj_weight,
    proj_bias,
    cotangent,
):
    T, D = tokens.shape
    G = segment_ids.shape[1]
    S, DP = lax.axis_size("sp"), lax.axis_size("dp")
    NX = math.isqrt(DP // 2)
    NZ = DP // NX
    NY = S // 2
    HW, FW = qkv_weight.shape[2] // S, in_weight.shape[1] // S
    DB, ZW = D // DP, D // NZ
    CW = FW
    nk = min(G, G // 2 + QB)
    FZ = FW // 4
    half = [10000.0 ** (-2.0 * f / ROT) for f in range(ROT // 2)]
    freq = jnp.asarray(np.tile(np.asarray(half, np.float32), LANES // len(half))[None, :])

    vm = pltpu.VMEM
    dma = pltpu.SemaphoreType.DMA
    scratch = dict(
        tok=vm((T, D), BF16), mean=vm((T, LANES), F32), inv=vm((T, LANES), F32),
        tab_c=vm((G, LANES), F32), tab_s=vm((G, LANES), F32), segc=vm((G, LANES), F32), nrm=vm((G, D), BF16), cot=vm((G, D), BF16),
        win=vm((D, FW), BF16), wproj=vm((FW, D), BF16), wqkv=vm((3, D, HW), BF16), wout=vm((HW, D), BF16),
        hid=vm((G, FW), BF16), dgel=vm((G, FW), F32), gpre=vm((G, FW), BF16),
        q=vm((G, HW), BF16), k=vm((G, HW), BF16), v=vm((G, HW), BF16), gm=vm((G, HW), BF16), mix=vm((G, HW), BF16),
        gk=vm((G, HW), F32), gv=vm((G, HW), F32), gq=vm((HW, QB), F32), mask=vm((nk, QB), F32),
        kt=vm((HW, G), BF16), vt=vm((HW, G), BF16),
        grads=vm((G, 3 * HW), BF16), lse=vm((8, G), F32),
        tmp=vm((max(ZW, T), CW), F32),
        acc=vm((3, NZ, DB, CW), F32), xs=vm((3, NZ, NX - 1, DB, CW), BF16), xr=vm((3, NZ, NX - 1, DB, CW), BF16),
        zr=vm((3, NZ + 1, DB, CW), BF16),
        za=vm((NZ, ZW, FZ), BF16), zb=vm((NZ + 1, ZW, FZ), BF16), zc=vm((NZ, ZW, FZ), F32),
        xa=vm((NX - 1, DB, FZ), BF16), xb=vm((NX - 1, DB, FZ), BF16),
        zas=dma((NZ,)), zbs=dma((NZ + 1,)), xas=dma((NX - 1,)), xbs=dma((NX - 1,)),
        keep=vm((2, NY, T, D), BF16), csend=vm((NY, T, D), BF16), crecv=vm((2, NY, T, D), BF16),
        ysend=vm((2, NY - 1, T, D), BF16), yrecv=vm((2, NY - 1, T, D), BF16),
        vacc=vm((4, 8, D), F32), v1=vm((2, 2, D), F32), v1r=vm((2, DP - 1, 2, D), F32),
        v2=vm((2, 2, D), F32), v2r=vm((2, S - 1, 2, D), F32),
        ld_sem=dma((6,)), ns=dma((2 * NY - 1,)), nr=dma((2 * NY - 1,)),
        cs=dma((NZ, 2 * NY - 1)), cr=dma((NZ, 2 * NY - 1)),
        xss=dma((3, NZ, NX - 1)), xrs=dma((3, NZ, NX - 1)), zss=dma((3, NZ)), zrs=dma((3, NZ + 1)),
        css=dma((2, NY)), crs=dma((2, NY)), yss=dma((2, NY - 1)), yrs=dma((2, NY - 1)),
        v1s=dma((2, DP - 1)), v1rs=dma((2, DP - 1)), v2s=dma((2, S - 1)), v2rs=dma((2, S - 1)),
    )
    in_vmem = pl.BlockSpec(memory_space=pltpu.VMEM)
    anywhere = pl.BlockSpec(memory_space=pl.ANY)
    sizes = dict(
        n_in=12, n_out=7, scratch=tuple(scratch), T=T, D=D, G=G, S=S, DP=DP, NX=NX, NZ=NZ, NY=NY,
        HW=HW, FW=FW, FZ=FZ, DB=DB, ZW=ZW, CW=CW,
    )
    shape = jax.ShapeDtypeStruct
    out, d_tokens, sum_p, sum_i, sum_a, vec, inb = pl.pallas_call(
        functools.partial(block_kernel, sizes),
        out_shape=(
            shape((T, D), BF16), shape((T, D), F32), shape((DB, CW), F32), shape((DB, CW), F32),
            shape((DB, CW), F32), shape((8, D), F32), shape((S, FW), F32),
        ),
        in_specs=[anywhere] * 2 + [in_vmem] * 6 + [anywhere] * 4,
        out_specs=(in_vmem,) * 7,
        scratch_shapes=list(scratch.values()),
        compiler_params=pltpu.CompilerParams(
            collective_id=0, has_side_effects=True, vmem_limit_bytes=67043328
        ),
        name="block",
    )(
        tokens, cotangent, segment_ids, freq, norm_gain[None, :], norm_bias[None, :],
        in_bias[None, :], proj_bias[None, :], qkv_weight, out_weight, in_weight, proj_weight,
    )
    parts = pl.pallas_call(
        functools.partial(place_kernel, HW, FW),
        out_shape=(
            shape((T, D), BF16), shape((T, D), F32), shape((1, D), F32), shape((1, D), F32),
            shape((3, DB, HW), F32), shape((HW, DB), F32), shape((DB, FW), F32), shape((1, S * FW), F32),
            shape((FW, DB), F32), shape((1, D), F32),
        ),
        in_specs=[in_vmem] * 7,
        out_specs=(in_vmem,) * 10,
        compiler_params=pltpu.CompilerParams(vmem_limit_bytes=67043328),
        name="place",
    )(out, d_tokens, sum_p, sum_i, sum_a, vec, inb)
    return tuple(p.reshape(-1) if p.shape[0] == 1 else p for p in parts)


def solution(mesh):
    placed = (
        P(("dp", "sp"), None), P("dp", None), P(), P(), P(), P(), P(), P(), P(), P(), P(("dp", "sp"), None),
    )
    return jax.shard_map(
        per_device,
        mesh=mesh,
        in_specs=placed,
        out_specs=(
            P(("dp", "sp"), None), P(("dp", "sp"), None), P(), P(), P(None, "dp", "sp"), P("sp", "dp"),
            P("dp", "sp"), P(), P("sp", "dp"), P(),
        ),
        check_vma=False,
    )
```
